512 devices in a mesh: sec: 4 (over z_lo), gx: 8 (over z_hi, x), gy: 16 (over y, core).
Axes of the slice: x: 4, y: 8, z: 8 (z_hi: 2, z_lo: 4; z = z_hi * 4 + z_lo), core: 2. Of those that a mesh axis runs over, the one named last changes fastest.
Arguments:
- soil_class: int32 [256, 4096], P('gx', 'gy'), may hold values from 0 to 11
- geology_class: int32 [256, 4096], P('gx', 'gy'), may hold values from 0 to 15
- land_mask: int32 [256, 4096], P('gx', 'gy'), may hold values 0 or 1
- river_mask: int32 [256, 4096], P('gx', 'gy'), may hold values 0 or 1
- elevation: float32 [256, 4096], P('gx', 'gy'), may hold values from -6 to 6
- roughness: float32 [256, 4096], P('gx', 'gy'), may hold values from 0.02 to 0.11
- rainfall: float32 [256, 4096], P('gx', 'gy'), may hold values from 0.05 to 1
- potential_evap: float32 [256, 4096], P('gx', 'gy'), may hold values from 0.05 to 0.5
- surface_head: float32 [256, 4096], P('gx', 'gy'), may hold values from -3 to 3
- pressure: float32 [8, 256, 4096], P('sec', 'gx', 'gy'), may hold values from -6 to 6
- storage: float32 [8, 256, 4096], P('sec', 'gx', 'gy'), may hold values from 0.2 to 2
- soil_embed: bfloat16 [12, 128], replicated, may hold values from -4 to 4
- geology_embed: bfloat16 [16, 128], replicated, may hold values from -4 to 4
- conv_weight: bfloat16 [3, 3, 128, 128], replicated, may hold values from -0.1875 to 0.1875
- out_weight: bfloat16 [128, 8], replicated, may hold values from -0.5 to 0.5
Outputs:
- pressure_out: float32 [8, 256, 4096], P('sec', 'gx', 'gy')
- head_out: float32 [256, 4096], P('gx', 'gy')
The draws below stay inside these ranges and needn't reach their ends.
All inputs are finite; a program needn't handle non-finite values. No bound on the sum of `land_mask` or of `river_mask` on one device may be relied on, other than what follows from the above.
Results may differ from the reference program's by a relative error of at most 0.0041.
Values sent between devices are 32-bit elements; how exact they have to be, the bound alone decides.
No kernel may reach another device: no remote copies, remote signals or barrier semaphores. Data moves between devices by JAX's collectives and lax.ppermute only.
A program may use at most 64 MiB of HBM per device.

```python
import math
import jax
import jax.numpy as jnp
from jax import lax

CX = 32
CHANNELS = 128
NSOIL = 12
NGEO = 16
SWEEPS = 4
CYCLES = 4
LAYERS = 8
NX = 256
NY = 4096
N_GX = 8


def set_ends(entries, rng, least, top_value):
    longest = entries.shape.index(max(entries.shape))
    spots = []
    for shift in (0, 1):
        where = [jax.random.randint(jax.random.fold_in(rng, axis), (), 0, length) for axis, length in enumerate(entries.shape)]
        where[longest] = (where[longest] + shift) % entries.shape[longest]
        spots.append(tuple(where))
    return entries.at[spots[0]].set(least).at[spots[1]].set(top_value)


def block_scale(stream_key, dims, pieces, least, high):
    gain = 1.0
    for axis_at, parts in pieces:
        draws = jax.random.uniform(jax.random.fold_in(jax.random.fold_in(stream_key, 6), axis_at), (parts,), jnp.float32, least / len(pieces), high / len(pieces))
        gain = gain * jnp.repeat(jnp.exp(draws), dims[axis_at] // parts).reshape((-1,) + (1,) * (len(dims) - 1 - axis_at))
    return gain


def gaussian(key, shape, width, limit, pieces=(), held_as=jnp.bfloat16):
    result = jax.random.normal(key, shape, jnp.float32) * width
    if len(pieces) > 0:
        result = block_scale(key, shape, pieces, -0.22, 0.18) * result
    return jnp.clip(result, min=-limit, max=limit).astype(held_as)


def setup_inputs(seed: int = 0) -> dict:
    streams_of = jax.random.split(jax.random.key(seed), 16)
    return {
        "soil_class": set_ends(jax.random.randint(streams_of[0], (NX, NY), 0, NSOIL), jax.random.fold_in(streams_of[0], 1), 0, NSOIL - 1).astype(jnp.int32),
        "geology_class": set_ends(jax.random.randint(streams_of[1], (NX, NY), 0, NGEO), jax.random.fold_in(streams_of[1], 1), 0, NGEO - 1).astype(jnp.int32),
        "land_mask": set_ends((jax.random.randint(streams_of[2], (NX, NY), 0, 5) < 4).astype(jnp.int32), jax.random.fold_in(streams_of[2], 1), 0, 1),
        "river_mask": set_ends((jax.random.randint(streams_of[3], (NX, NY), 0, 8) < 1).astype(jnp.int32), jax.random.fold_in(streams_of[3], 1), 0, 1),
        "elevation": gaussian(streams_of[4], (NX, NY), 1.0, 6.0, ((0, 8), (1, 16)), jnp.float32),
        "roughness": jnp.clip(jnp.exp(math.log(0.11) - 1.7047481 * jax.random.uniform(streams_of[5], (NX, NY), jnp.float32) ** block_scale(streams_of[5], (NX, NY), ((0, 8), (1, 16)), -0.2, 0.2)), 0.02, 0.11),
        "rainfall": jnp.clip(jnp.exp(math.log(1.0) - 2.9957323 * jax.random.uniform(streams_of[6], (NX, NY), jnp.float32) ** block_scale(streams_of[6], (NX, NY), ((0, 8), (1, 16)), -0.2, 0.2)), 0.05, 1.0),
        "potential_evap": jnp.clip(jnp.exp(math.log(0.5) - 2.3025851 * jax.random.uniform(streams_of[7], (NX, NY), jnp.float32) ** block_scale(streams_of[7], (NX, NY), ((0, 8), (1, 16)), -0.2, 0.2)), 0.05, 0.5),
        "surface_head": gaussian(streams_of[8], (NX, NY), 0.5, 3.0, ((0, 8), (1, 16)), jnp.float32),
        "pressure": gaussian(streams_of[9], (LAYERS, NX, NY), 1.0, 6.0, ((0, 4), (1, 8), (2, 16)), jnp.float32),
        "storage": jnp.clip(jnp.exp(math.log(2.0) - 2.3025851 * jax.random.uniform(streams_of[10], (LAYERS, NX, NY), jnp.float32) ** block_scale(streams_of[10], (LAYERS, NX, NY), ((0, 4), (1, 8), (2, 16)), -0.2, 0.2)), 0.2, 2.0),
        "soil_embed": gaussian(streams_of[11], (NSOIL, CHANNELS), 1.0, 4.0),
        "geology_embed": gaussian(streams_of[12], (NGEO, CHANNELS), 1.0, 4.0),
        "conv_weight": gaussian(streams_of[13], (3, 3, CHANNELS, CHANNELS), (9 * CHANNELS) ** -0.5, 0.1875),
        "out_weight": gaussian(streams_of[14], (CHANNELS, LAYERS), CHANNELS ** -0.5, 0.5),
    }


infil_rate = 0.3
lateral = 1.0
vertical = 0.5


def infiltration(land_frac, top_cond, surface, top_press):
    return land_frac * (infil_rate * top_cond / (1.0 + top_cond)) * (surface - top_press)


def evaporation_loss(land_frac, potential, top_press):
    return land_frac * potential * jax.nn.sigmoid(top_press)


def surface_flux(level_pad, rough_pad):
    centre_level = level_pad[1:-1, 1:-1]
    centre_rough = rough_pad[1:-1, 1:-1]
    total = jnp.zeros_like(centre_level)
    pairs = ((level_pad[2:, 1:-1], rough_pad[2:, 1:-1]), (level_pad[:-2, 1:-1], rough_pad[:-2, 1:-1]),
             (level_pad[1:-1, 2:], rough_pad[1:-1, 2:]), (level_pad[1:-1, :-2], rough_pad[1:-1, :-2]))
    for near_level, near_rough in pairs:
        total = total + 0.5 * (centre_rough + near_rough) * (near_level - centre_level)
    return total


def shifted(values):
    return [(values[:-2, 1:-1, 1:-1], vertical), (values[2:, 1:-1, 1:-1], vertical),
            (values[1:-1, :-2, 1:-1], lateral), (values[1:-1, 2:, 1:-1], lateral),
            (values[1:-1, 1:-1, 2:], lateral), (values[1:-1, 1:-1, :-2], lateral)]


def jacobi_sweep(press_pad, cond_pad, rhs_mid, store_mid):
    cond_mid = cond_pad[1:-1, 1:-1, 1:-1]
    diagonal = store_mid
    total = rhs_mid
    for (near_press, factor), (near_cond, unused) in zip(shifted(press_pad), shifted(cond_pad)):
        face = factor * 0.5 * (cond_mid + near_cond)
        diagonal = diagonal + face
        total = total + face * near_press
    return total / diagonal


def reference(soil_class, geology_class, land_mask, river_mask, elevation, roughness, rainfall, potential_evap,
              surface_head, pressure, storage, soil_embed, geology_embed, conv_weight, out_weight):
    soil_pad = jnp.pad(soil_class, 1, constant_values=-1)
    geology_pad = jnp.pad(geology_class, 1, constant_values=-1)
    soil_table = soil_embed.astype(jnp.float32)
    geology_table = geology_embed.astype(jnp.float32)
    kernel = conv_weight.astype(jnp.float32)
    projection = out_weight.astype(jnp.float32)

    def block_logits(index):
        start = (index * CX).astype(jnp.int32)
        soil_rows = lax.dynamic_slice_in_dim(soil_pad, start, CX + 2, 0)
        geology_rows = lax.dynamic_slice_in_dim(geology_pad, start, CX + 2, 0)
        soil_onehot = (soil_rows[:, :, None] == jnp.arange(NSOIL, dtype=jnp.int32)).astype(jnp.float32)
        geology_onehot = (geology_rows[:, :, None] == jnp.arange(NGEO, dtype=jnp.int32)).astype(jnp.float32)
        features = jnp.einsum("xys,sc->xyc", soil_onehot, soil_table) + jnp.einsum("xys,sc->xyc", geology_onehot, geology_table)
        features = features.astype(jnp.bfloat16).astype(jnp.float32)
        convolved = lax.conv_general_dilated(features[None], kernel, (1, 1), "VALID",
                                             dimension_numbers=("NHWC", "HWIO", "NCHW"),
                                             precision=lax.Precision.HIGHEST)[0]
        hidden = jax.nn.relu(convolved).astype(jnp.bfloat16).astype(jnp.float32)
        return jnp.einsum("cxy,cl->lxy", hidden, projection)

    blocks = lax.map(block_logits, jnp.arange(N_GX, dtype=jnp.int32))
    logits = jnp.transpose(blocks, (1, 0, 2, 3)).reshape(LAYERS, NX, NY)
    conduct = jnp.exp(logits)

    land_frac = land_mask.astype(jnp.float32)
    river_frac = river_mask.astype(jnp.float32)
    rough = land_frac * (1.0 + river_frac) * roughness
    rough_pad = jnp.pad(rough, 1)
    cond_pad = jnp.pad(conduct, 1)
    top_layer = (jnp.arange(LAYERS, dtype=jnp.int32) == 0).astype(jnp.float32)[:, None, None]
    surface = surface_head
    press = pressure
    for cycle in range(CYCLES):
        top_press = press[0]
        infil = infiltration(land_frac, conduct[0], surface, top_press)
        evap = evaporation_loss(land_frac, potential_evap, top_press)
        flux = surface_flux(jnp.pad(surface + elevation, 1), rough_pad)
        surface = surface + land_frac * (rainfall - infil + flux)
        source = infil - evap
        rhs = storage * press + top_layer * source[None]
        for sweep in range(SWEEPS):
            press = jacobi_sweep(jnp.pad(press, 1), cond_pad, rhs, storage)
    return press, surface
```

```python
import functools

import jax
import jax.numpy as jnp
import numpy as np
from jax import lax
from jax.experimental import pallas as pl
from jax.experimental.pallas import tpu as pltpu
from jax.sharding import PartitionSpec as P

SWEEPS = 4
CYCLES = 4
HALO = SWEEPS * CYCLES
LANES = 128
CHUNK = 64
EDGE = (LANES - CHUNK) // 2
CROWS = 24
NSOIL = 12
NGEO = 16
KSOIL = 9 * NGEO
KROWS = 256

infil_rate = 0.3
lateral = 1.0
vertical = 0.5

VMEM = pl.BlockSpec(memory_space=pltpu.VMEM)
SMEM = pl.BlockSpec(memory_space=pltpu.SMEM)
f32 = jnp.float32
bf16 = jnp.bfloat16


def call(kernel, outs, n_in, scratch=(), smem=(), name=None):
    return pl.pallas_call(
        kernel,
        out_shape=outs,
        in_specs=[SMEM if i in smem else VMEM for i in range(n_in)],
        out_specs=jax.tree.map(lambda _: VMEM, outs),
        scratch_shapes=scratch,
        name=name,
    )


def swap_pairs(count, first):
    out = []
    for i in range(first, count - 1, 2):
        out += [(i, i + 1), (i + 1, i)]
    return out


def table_layout():
    sel = np.zeros((KROWS, NSOIL + NGEO), np.float32)
    tap = np.full((KROWS, LANES), -1, np.int32)
    for k in range(KSOIL):
        sel[k, NSOIL + k % NGEO] = 1
        tap[k] = k // NGEO
    for j in range(9 * NSOIL):
        sel[KSOIL + j, j % NSOIL] = 1
        tap[KSOIL + j] = j // NSOIL
    return sel, tap


def table_kernel(sel_ref, tap_ref, soil_ref, geo_ref, weight_ref, out_ref, table_ref, proj_ref):
    sel = sel_ref[...].astype(bf16)
    embed = jnp.dot(sel[:, :NSOIL], soil_ref[...], preferred_element_type=f32)
    embed = embed + jnp.dot(sel[:, NSOIL:], geo_ref[...], preferred_element_type=f32)
    tap = tap_ref[...]
    total = jnp.zeros((LANES, KROWS), f32)
    for t in range(9):
        mine = jnp.where(tap == t, embed, 0.0).astype(bf16)
        total = total + lax.dot_general(
            weight_ref[t], mine, (((0,), (1,)), ((), ())), preferred_element_type=f32
        )
    high = total.astype(bf16)
    table_ref[0:LANES, :] = high
    table_ref[LANES : 2 * LANES, :] = (total - high.astype(f32)).astype(bf16)
    eye = (
        lax.broadcasted_iota(jnp.int32, (LANES, LANES), 0)
        == lax.broadcasted_iota(jnp.int32, (LANES, LANES), 1)
    ).astype(f32).astype(bf16)
    proj_ref[...] = lax.dot_general(
        out_ref[...], eye, (((0,), (0,)), ((), ())), preferred_element_type=f32
    ).astype(bf16)


def columns(soil, geo, land, river, elev, rough, rain, evap, head):
    landf = land.astype(f32)
    conveyance = landf * (1.0 + river.astype(f32)) * rough
    return (
        [conveyance, rain, evap, elev, head],
        [(soil + 1).astype(f32), (geo + 1).astype(f32)],
    )


def pack_cols_kernel(
    par_ref, soil, geo, land, river, elev, rough, rain, evap, head, press, stor, a_ref, b_ref
):
    odd = par_ref[0] == 1
    plain, classes = columns(
        soil[...], geo[...], land[...], river[...], elev[...], rough[...], rain[...], evap[...], head[...]
    )
    plain = [press[0], press[1], stor[0], stor[1]] + plain
    width = plain[0].shape[1]
    lane = lax.broadcasted_iota(jnp.int32, (plain[0].shape[0], LANES), 1)

    def side(right):
        halves = []
        for half in range(2):
            acc = jnp.zeros((plain[0].shape[0], LANES), f32)
            items = []
            if half == 0:
                items = [(plain[i], 16, 16 * i) for i in range(8)]
            else:
                items = [(plain[8], 16, 0), (classes[0], 32, 32), (classes[1], 32, 64)]
            for value, wide, at in items:
                part = value[:, width - LANES :] if right else value[:, :LANES]
                start = LANES - wide if right else 0
                moved = part if start == at else pltpu.roll(part, (at - start) % LANES, 1)
                acc = jnp.where((lane >= at) & (lane < at + wide), moved, acc)
            halves.append(acc)
        return halves

    left, right = side(False), side(True)
    for half in range(2):
        cols = slice(half * LANES, (half + 1) * LANES)
        a_ref[:, cols] = jnp.where(odd, left[half], right[half])
        b_ref[:, cols] = jnp.where(odd, right[half], left[half])


def slice_kernel(
    par_ref, soil, geo, land, river, elev, rough, rain, evap, head, press, stor, a_ref, b_ref,
    z_ref, c_ref, work_ref,
):
    odd = par_ref[0] == 1
    plain, classes = columns(
        soil[...], geo[...], land[...], river[...], elev[...], rough[...], rain[...], evap[...], head[...]
    )
    plain = [press[0], press[1], stor[0], stor[1]] + plain
    rows, width = plain[0].shape
    lane = lax.broadcasted_iota(jnp.int32, (rows, LANES), 1)
    got_a, got_b = a_ref[...], b_ref[...]
    left = jnp.where(odd, got_a, got_b)
    right = jnp.where(odd, got_b, got_a)

    def slices(value, half, at, wide):
        cols = slice(half * LANES, (half + 1) * LANES)
        lo, hi = left[:, cols], right[:, cols]
        move = (EDGE - wide - at) % LANES
        lo = pltpu.roll(lo, move, 1) if move else lo
        move = (LANES - EDGE - at) % LANES
        hi = pltpu.roll(hi, move, 1) if move else hi
        first, last = value[:, :LANES], value[:, width - LANES :]
        low_r, high_r = pltpu.roll(first, EDGE, 1), pltpu.roll(last, EDGE, 1)
        low_l, high_l = pltpu.roll(first, LANES - EDGE, 1), pltpu.roll(last, LANES - EDGE, 1)
        zero = jnp.zeros_like(lo)
        return [
            jnp.where(lane < EDGE, jnp.where(lane >= EDGE - wide, lo, zero), low_r),
            jnp.where(lane < LANES - EDGE, low_l, high_l),
            jnp.where(lane < EDGE, low_r, high_r),
            jnp.where(lane < LANES - EDGE, high_l, jnp.where(lane < LANES - EDGE + wide, hi, zero)),
        ]

    for i in range(4):
        for d, part in enumerate(slices(plain[i], 0, 16 * i, 16)):
            z_ref[d, i] = part
    spots = [(0, 16 * i, 16) for i in range(4, 8)] + [(1, 0, 16), (1, 32, 32), (1, 64, 32)]
    for j, (value, (half, at, wide)) in enumerate(zip(plain[4:] + classes, spots)):
        for d, part in enumerate(slices(value, half, at, wide)):
            work_ref[d, j] = part
    c_ref[...] = work_ref[par_ref[1]]


def pack_rows_kernel(par_ref, z_ref, c_ref, a_ref, b_ref):
    odd = par_ref[0] == 1
    rows = z_ref.shape[2]
    low = jnp.where(odd, rows - HALO, 0)
    low_class = jnp.where(odd, rows - CROWS, 0)
    for ref, at, at_class in (
        (a_ref, low, low_class),
        (b_ref, (rows - HALO) - low, (rows - CROWS) - low_class),
    ):
        at = pl.multiple_of(at, 8)
        at_class = pl.multiple_of(at_class, 8)
        for s in range(4):
            for i in range(4):
                k = 8 * (i // 2) + 2 * s + i % 2
                ref[pl.ds(k * HALO, HALO), :] = z_ref[s, i, pl.ds(at, HALO), :]
        for j in range(5):
            ref[pl.ds((16 + j) * HALO, HALO), :] = c_ref[j, pl.ds(at, HALO), :]
        for j in range(2):
            ref[pl.ds(21 * HALO + j * CROWS, CROWS), :] = c_ref[5 + j, pl.ds(at_class, CROWS), :]


MSG_ROWS = 21 * HALO + 2 * CROWS


def main_kernel(
    par_ref, z_ref, c_ref, a_ref, b_ref, table_ref, proj_ref, out_ref,
    top_ref, bot_ref, shift_ref, cond_ref, press_ref, press2_ref, stor_ref, coef_ref, rhs_ref, flat_ref, src_ref,
):
    odd = par_ref[0] == 1
    rows = z_ref.shape[2]
    full = rows + 2 * HALO
    full_class = rows + 2 * CROWS
    top_ref[...] = jnp.where(odd, b_ref[...], a_ref[...])
    bot_ref[...] = jnp.where(odd, a_ref[...], b_ref[...])

    for j in range(2):
        at = 21 * HALO + j * CROWS
        value = jnp.concatenate([top_ref[at : at + CROWS, :], c_ref[5 + j], bot_ref[at : at + CROWS, :]], axis=0)
        for dx in (-1, 0, 1):
            shift_ref[(3 * j + dx + 1), :, :] = (pltpu.roll(value, (-dx) % LANES, 1) if dx else value) - 1.0

    for j in range(5):
        at = (16 + j) * HALO
        flat_ref[j, 0:HALO, :] = top_ref[at : at + HALO, :]
        flat_ref[j, HALO : HALO + rows, :] = c_ref[j]
        flat_ref[j, HALO + rows : full, :] = bot_ref[at : at + HALO, :]

    for f, ref in ((0, press_ref), (1, stor_ref)):
        for r in range(0, full, 8):
            parts = []
            for l in range(8):
                k = 8 * f + l
                if r < HALO:
                    part = top_ref[k * HALO + r : k * HALO + r + 8, :]
                elif r < HALO + rows:
                    part = z_ref[l // 2, 2 * f + l % 2, r - HALO : r - HALO + 8, :]
                else:
                    at = k * HALO + r - HALO - rows
                    part = bot_ref[at : at + 8, :]
                parts.append(part)
            ref[r : r + 8] = jnp.swapaxes(jnp.stack(parts), 0, 1)

    sub = lax.broadcasted_iota(jnp.int32, (8, LANES), 0)
    geo_low = sub.astype(f32)
    geo_high = geo_low + 8.0
    soil_mid = jnp.where(sub < 4, sub + 8, sub - 4).astype(f32)
    soil_late = (sub + 4).astype(f32)
    first4 = sub < 4

    def one_hot(row):
        def spread(kind, t):
            dy, dx = t // 3 - 1, t % 3
            return jnp.broadcast_to(shift_ref[3 * kind + dx, pl.ds(row + dy, 1), :], (8, LANES))

        tiles = []
        for t in range(9):
            value = spread(1, t)
            tiles += [value == geo_low, value == geo_high]
        soils = [spread(0, t) for t in range(9)]
        t = 0
        while t < 9:
            tiles.append(soils[t] == geo_low)
            if t + 1 < 9:
                tiles.append(jnp.where(first4, soils[t], soils[t + 1]) == soil_mid)
                tiles.append(soils[t + 1] == soil_late)
            else:
                tiles.append(jnp.where(first4, soils[t], -9.0) == soil_mid)
            t += 2
        pairs = [
            jnp.concatenate([jnp.where(a, 1.0, 0.0), jnp.where(b, 1.0, 0.0)], axis=0).astype(bf16)
            for a, b in zip(tiles[0::2], tiles[1::2])
        ]
        return jnp.concatenate(pairs, axis=0)

    table = table_ref[...]
    proj = proj_ref[...]

    def conduct_pair(i, carry):
        row = 2 * i
        at = row + CROWS - HALO
        hot = jnp.concatenate([one_hot(at), one_hot(at + 1)], axis=1)
        both = jnp.dot(table, hot, preferred_element_type=f32)
        hidden = jnp.maximum(both[:LANES] + both[LANES:], 0.0).astype(bf16)
        logits = jnp.dot(proj, hidden, preferred_element_type=f32)
        value = jnp.exp(logits)
        for k in range(2):
            inside = jnp.broadcast_to(shift_ref[1, pl.ds(at + k, 1), :], (8, LANES)) >= 0.0
            cond_ref[row + k] = jnp.where(inside, value[:, k * LANES : (k + 1) * LANES], 0.0)
        return carry

    lax.fori_loop(0, full // 2, conduct_pair, 0)

    def coefficients(r, carry):
        mid = cond_ref[r]
        north = 0.5 * lateral * (mid + cond_ref[r - 1])
        south = 0.5 * lateral * (mid + cond_ref[r + 1])
        east = 0.5 * lateral * (mid + pltpu.roll(mid, LANES - 1, 1))
        west = 0.5 * lateral * (mid + pltpu.roll(mid, 1, 1))
        up = 0.5 * vertical * (mid + jnp.where(sub > 0, pltpu.roll(mid, 1, 0), 0.0))
        down = 0.5 * vertical * (mid + jnp.where(sub < 7, pltpu.roll(mid, 7, 0), 0.0))
        store = stor_ref[r]
        diagonal = store + up + down + north + south + east + west
        live = store > 0.0
        inverse = jnp.where(live, 1.0, 0.0) / jnp.where(live, diagonal, 1.0)
        coef_ref[0, r] = jnp.where(sub > 0, up * inverse, 0.0)
        coef_ref[1, r] = jnp.where(sub < 7, down * inverse, 0.0)
        coef_ref[2, r] = north * inverse
        coef_ref[3, r] = south * inverse
        coef_ref[4, r] = east * inverse
        coef_ref[5, r] = west * inverse
        coef_ref[6, r] = store * inverse
        coef_ref[7, r] = jnp.where(sub == 0, inverse, 0.0)
        return carry

    lax.fori_loop(1, full - 1, coefficients, 0)

    rough, rain, evap, elev = flat_ref[0], flat_ref[1], flat_ref[2], flat_ref[3]
    head = flat_ref[4]
    land = jnp.where(rough > 0.0, 1.0, 0.0)

    def around(value):
        return (
            pltpu.roll(value, full - 1, 0),
            pltpu.roll(value, 1, 0),
            pltpu.roll(value, LANES - 1, 1),
            pltpu.roll(value, 1, 1),
        )

    faces = [0.5 * (rough + near) for near in around(rough)]
    top_cond = jnp.concatenate([cond_ref[r, 0:1, :] for r in range(full)], axis=0)
    rate = land * (infil_rate * top_cond / (1.0 + top_cond))
    loss = land * evap
    for cycle in range(CYCLES):
        top = jnp.concatenate([press_ref[r, 0:1, :] for r in range(full)], axis=0)
        level = head + elev
        flux = jnp.zeros_like(level)
        for face, near in zip(faces, around(level)):
            flux = flux + face * (near - level)
        infil = rate * (head - top)
        src_ref[...] = infil - loss * jax.nn.sigmoid(top)
        head = head + land * (rain - infil + flux)
        done = cycle * SWEEPS

        def right_side(r, carry):
            source = jnp.broadcast_to(src_ref[pl.ds(r, 1), :], (8, LANES))
            rhs_ref[r] = coef_ref[6, r] * press_ref[r] + coef_ref[7, r] * source
            return carry

        lax.fori_loop(done + 1, full - 1 - done, right_side, 0)
        for sweep in range(SWEEPS):
            old, new = (press_ref, press2_ref) if sweep % 2 == 0 else (press2_ref, press_ref)

            def one_row(r, carry):
                north, mid = carry
                south = old[r + 1]
                total = rhs_ref[r] + coef_ref[0, r] * pltpu.roll(mid, 1, 0)
                total = total + coef_ref[1, r] * pltpu.roll(mid, 7, 0)
                total = total + coef_ref[2, r] * north
                total = total + coef_ref[3, r] * south
                total = total + coef_ref[4, r] * pltpu.roll(mid, LANES - 1, 1)
                total = total + coef_ref[5, r] * pltpu.roll(mid, 1, 1)
                new[r] = total
                return mid, south

            first = done + sweep + 1
            lax.fori_loop(first, full - first, one_row, (old[first - 1], old[first]), unroll=2)

    lane = lax.broadcasted_iota(jnp.int32, (8, LANES), 1)
    for r in range(HALO, HALO + rows, 8):
        layers = jnp.swapaxes(press_ref[r : r + 8], 0, 1)
        for s in range(4):
            out_ref[s, 0, r - HALO : r - HALO + 8, :] = jnp.where(
                lane < CHUNK,
                pltpu.roll(layers[2 * s], LANES - EDGE, 1),
                pltpu.roll(layers[2 * s + 1], EDGE, 1),
            )
            out_ref[s, 1, r - HALO : r - HALO + 8, :] = pltpu.roll(head[r : r + 8], LANES - EDGE, 1)


def finish_kernel(z_ref, press_ref, head_ref):
    rows = z_ref.shape[2]
    lane = lax.broadcasted_iota(jnp.int32, (rows, LANES), 1)
    for d in range(0, 4, 2):
        cols = slice(d * CHUNK, d * CHUNK + LANES)
        a, b = z_ref[d, 0], z_ref[d + 1, 0]
        press_ref[0, :, cols] = jnp.where(lane < CHUNK, a, pltpu.roll(b, CHUNK, 1))
        press_ref[1, :, cols] = jnp.where(lane < CHUNK, pltpu.roll(a, CHUNK, 1), b)
        head_ref[:, cols] = jnp.where(lane < CHUNK, z_ref[d, 1], pltpu.roll(z_ref[d + 1, 1], CHUNK, 1))


def shards(
    soil_class, geology_class, land_mask, river_mask, elevation, roughness, rainfall, potential_evap,
    surface_head, pressure, storage, soil_embed, geology_embed, conv_weight, out_weight,
):
    rows, width = soil_class.shape
    sec = lax.axis_index("sec")
    gx = lax.axis_index("gx")
    gy = lax.axis_index("gy")
    n_gx, n_gy = lax.axis_size("gx"), lax.axis_size("gy")
    full = rows + 2 * HALO
    sds = jax.ShapeDtypeStruct
    raw = (
        soil_class, geology_class, land_mask, river_mask, elevation, roughness, rainfall,
        potential_evap, surface_head, pressure, storage,
    )
    par_y = jnp.stack([gy % 2, sec]).astype(jnp.int32)
    par_x = jnp.stack([gx % 2, sec]).astype(jnp.int32)

    sel, tap = table_layout()
    table, proj = call(
        table_kernel, (sds((2 * LANES, KROWS), bf16), sds((out_weight.shape[1], LANES), bf16)), 6, name="table"
    )(
        jnp.asarray(sel), jnp.asarray(tap), soil_embed, geology_embed,
        conv_weight.reshape(9, LANES, LANES), out_weight,
    )

    edge = sds((rows, 2 * LANES), f32)
    ya, yb = call(pack_cols_kernel, (edge, edge), 12, smem=(0,), name="pack_cols")(par_y, *raw)
    ya = lax.ppermute(ya, "gy", swap_pairs(n_gy, 0))
    yb = lax.ppermute(yb, "gy", swap_pairs(n_gy, 1))
    z, cols = call(
        slice_kernel, (sds((4, 4, rows, LANES), f32), sds((7, rows, LANES), f32)), 14,
        scratch=[pltpu.VMEM((4, 7, rows, LANES), f32)], smem=(0,), name="slices",
    )(par_y, *raw, ya, yb)
    z = lax.all_to_all(z, "sec", 0, 0)
    msg = sds((MSG_ROWS, LANES), f32)
    xa, xb = call(pack_rows_kernel, (msg, msg), 3, smem=(0,), name="pack_rows")(par_x, z, cols)
    xa = lax.ppermute(xa, "gx", swap_pairs(n_gx, 1))
    xb = lax.ppermute(xb, "gx", swap_pairs(n_gx, 0))
    grid = (full, 8, LANES)
    out = call(
        main_kernel, sds((4, 2, rows, LANES), f32), 7,
        scratch=[
            pltpu.VMEM((MSG_ROWS, LANES), f32),
            pltpu.VMEM((MSG_ROWS, LANES), f32),
            pltpu.VMEM((6, rows + 2 * CROWS, LANES), f32),
            pltpu.VMEM(grid, f32),
            pltpu.VMEM(grid, f32),
            pltpu.VMEM(grid, f32),
            pltpu.VMEM(grid, f32),
            pltpu.VMEM((8,) + grid, f32),
            pltpu.VMEM(grid, f32),
            pltpu.VMEM((5, full, LANES), f32),
            pltpu.VMEM((full, LANES), f32),
        ],
        smem=(0,), name="cycles",
    )(par_x, z, cols, xa, xb, table, proj)
    out = lax.all_to_all(out, "sec", 0, 0)
    return tuple(
        call(finish_kernel, (sds(pressure.shape, f32), sds((rows, width), f32)), 1, name="finish")(out)
    )


def solution(mesh):
    flat = P("gx", "gy")
    deep = P("sec", "gx", "gy")
    in_specs = (flat,) * 9 + (deep, deep) + (P(),) * 4
    return jax.shard_map(shards, mesh=mesh, in_specs=in_specs, out_specs=(deep, flat), check_vma=False)
```

```python
import functools

import jax
import jax.numpy as jnp
import numpy as np
from jax import lax
from jax.experimental import pallas as pl
from jax.experimental.pallas import tpu as pltpu
from jax.sharding import PartitionSpec as P

SWEEPS = 4
CYCLES = 4
HALO = SWEEPS * CYCLES
LANES = 128
CHUNK = 64
EDGE = (LANES - CHUNK) // 2
CROWS = 24
NSOIL = 12
NGEO = 16
KSOIL = 9 * NGEO
KROWS = 256

infil_rate = 0.3
lateral = 1.0
vertical = 0.5

VMEM = pl.BlockSpec(memory_space=pltpu.VMEM)
f32 = jnp.float32
bf16 = jnp.bfloat16


def call(kernel, outs, args, scratch=(), name=None, hbm=(), final=False):
    made = outs if final else tuple(pltpu.VMEM(o.shape, o.dtype) for o in outs)
    args = [x if i in hbm else pltpu.with_memory_space_constraint(x, pltpu.VMEM) for i, x in enumerate(args)]
    return pl.pallas_call(
        kernel,
        out_shape=made,
        in_specs=[VMEM] * len(args),
        out_specs=tuple(VMEM for _ in outs),
        scratch_shapes=scratch,
        name=name,
    )(*args)


def swap_pairs(count, first):
    out = []
    for i in range(first, count - 1, 2):
        out += [(i, i + 1), (i + 1, i)]
    return out


def table_layout():
    sel = np.zeros((KROWS, NSOIL + NGEO), np.float32)
    tap = np.full((KROWS, LANES), -1, np.int32)
    for k in range(KSOIL):
        sel[k, NSOIL + k % NGEO] = 1
        tap[k] = k // NGEO
    for j in range(9 * NSOIL):
        sel[KSOIL + j, j % NSOIL] = 1
        tap[KSOIL + j] = j // NSOIL
    return sel, tap


def table_kernel(sel_ref, tap_ref, soil_ref, geo_ref, weight_ref, table_ref):
    sel = sel_ref[...].astype(bf16)
    embed = jnp.dot(sel[:, :NSOIL], soil_ref[...], preferred_element_type=f32)
    embed = embed + jnp.dot(sel[:, NSOIL:], geo_ref[...], preferred_element_type=f32)
    tap = tap_ref[...]
    total = jnp.zeros((LANES, KROWS), f32)
    for t in range(9):
        mine = jnp.where(tap == t, embed, 0.0).astype(bf16)
        total = total + lax.dot_general(
            weight_ref[t], mine, (((0,), (1,)), ((), ())), preferred_element_type=f32
        )
    high = total.astype(bf16)
    table_ref[0:LANES, :] = high
    table_ref[LANES : 2 * LANES, :] = (total - high.astype(f32)).astype(bf16)


def columns(soil, geo, land, river, elev, rough, rain, evap, head):
    landf = land.astype(f32)
    conveyance = landf * (1.0 + river.astype(f32)) * rough
    return (
        [conveyance, rain, evap, elev, head],
        [(soil + 1).astype(f32), (geo + 1).astype(f32)],
    )


def pack_cols_kernel(
    soil, geo, land, river, elev, rough, rain, evap, head, press, stor, a_ref, b_ref
):
    odd = lax.axis_index("gy") % 2 == 1
    plain, classes = columns(
        soil[...], geo[...], land[...], river[...], elev[...], rough[...], rain[...], evap[...], head[...]
    )
    plain = [press[0], press[1], stor[0], stor[1]] + plain
    width = plain[0].shape[1]
    lane = lax.broadcasted_iota(jnp.int32, (plain[0].shape[0], LANES), 1)

    def side(right):
        halves = []
        for half in range(2):
            acc = jnp.zeros((plain[0].shape[0], LANES), f32)
            items = []
            if half == 0:
                items = [(plain[i], 16, 16 * i) for i in range(8)]
            else:
                items = [(plain[8], 16, 0), (classes[0], 32, 32), (classes[1], 32, 64)]
            for value, wide, at in items:
                part = value[:, width - LANES :] if right else value[:, :LANES]
                start = LANES - wide if right else 0
                moved = part if start == at else pltpu.roll(part, (at - start) % LANES, 1)
                acc = jnp.where((lane >= at) & (lane < at + wide), moved, acc)
            halves.append(acc)
        return halves

    left, right = side(False), side(True)
    for half in range(2):
        cols = slice(half * LANES, (half + 1) * LANES)
        a_ref[:, cols] = jnp.where(odd, left[half], right[half])
        b_ref[:, cols] = jnp.where(odd, right[half], left[half])


def slice_kernel(
    soil, geo, land, river, elev, rough, rain, evap, head, press, stor, a_ref, b_ref,
    z_ref, c_ref, work_ref,
):
    odd = lax.axis_index("gy") % 2 == 1
    plain, classes = columns(
        soil[...], geo[...], land[...], river[...], elev[...], rough[...], rain[...], evap[...], head[...]
    )
    plain = [press[0], press[1], stor[0], stor[1]] + plain
    rows, width = plain[0].shape
    lane = lax.broadcasted_iota(jnp.int32, (rows, LANES), 1)
    got_a, got_b = a_ref[...], b_ref[...]
    left = jnp.where(odd, got_a, got_b)
    right = jnp.where(odd, got_b, got_a)

    def slices(value, half, at, wide):
        cols = slice(half * LANES, (half + 1) * LANES)
        lo, hi = left[:, cols], right[:, cols]
        move = (EDGE - wide - at) % LANES
        lo = pltpu.roll(lo, move, 1) if move else lo
        move = (LANES - EDGE - at) % LANES
        hi = pltpu.roll(hi, move, 1) if move else hi
        first, last = value[:, :LANES], value[:, width - LANES :]
        low_r, high_r = pltpu.roll(first, EDGE, 1), pltpu.roll(last, EDGE, 1)
        low_l, high_l = pltpu.roll(first, LANES - EDGE, 1), pltpu.roll(last, LANES - EDGE, 1)
        zero = jnp.zeros_like(lo)
        return [
            jnp.where(lane < EDGE, jnp.where(lane >= EDGE - wide, lo, zero), low_r),
            jnp.where(lane < LANES - EDGE, low_l, high_l),
            jnp.where(lane < EDGE, low_r, high_r),
            jnp.where(lane < LANES - EDGE, high_l, jnp.where(lane < LANES - EDGE + wide, hi, zero)),
        ]

    for i in range(4):
        for d, part in enumerate(slices(plain[i], 0, 16 * i, 16)):
            z_ref[d, i] = part
    spots = [(0, 16 * i, 16) for i in range(4, 8)] + [(1, 0, 16), (1, 32, 32), (1, 64, 32)]
    for j, (value, (half, at, wide)) in enumerate(zip(plain[4:] + classes, spots)):
        for d, part in enumerate(slices(value, half, at, wide)):
            work_ref[d, j] = part
    c_ref[...] = work_ref[lax.axis_index("sec")]


def pack_rows_kernel(z_ref, c_ref, a_ref, b_ref):
    odd = lax.axis_index("gx") % 2 == 1
    rows = z_ref.shape[2]
    low = jnp.where(odd, rows - HALO, 0)
    low_class = jnp.where(odd, rows - CROWS, 0)
    for ref, at, at_class in (
        (a_ref, low, low_class),
        (b_ref, (rows - HALO) - low, (rows - CROWS) - low_class),
    ):
        at = pl.multiple_of(at, 8)
        at_class = pl.multiple_of(at_class, 8)
        for s in range(4):
            for i in range(4):
                k = 8 * (i // 2) + 2 * s + i % 2
                ref[pl.ds(k * HALO, HALO), :] = z_ref[s, i, pl.ds(at, HALO), :]
        for j in range(5):
            ref[pl.ds((16 + j) * HALO, HALO), :] = c_ref[j, pl.ds(at, HALO), :]
        for j in range(2):
            ref[pl.ds(21 * HALO + j * CROWS, CROWS), :] = c_ref[5 + j, pl.ds(at_class, CROWS), :]


MSG_ROWS = 21 * HALO + 2 * CROWS


STEP_S = 8
TRIPS_S = 1
BLOCK_K = 16
UNROLL_C = 3
UNROLL_OWN = 7
OWN = 2


def at_row(r):
    return pl.ds(pl.multiple_of(8 * r + 8, 8), 8)


def place(ref, r):
    return ref.at[at_row(r), :]


def beside(ref, mid, r, step):
    return pltpu.roll(mid, (-step) % 8, 0)


def row_blocks(low, high, size, body):
    assert (high - low) % size == 0

    def step(b, carry):
        for i in range(size):
            body(low + b * size + i)
        return carry

    lax.fori_loop(0, (high - low) // size, step, 0)


def shift_classes(ref, kind, value):
    for dx in (-1, 0, 1):
        ref[3 * kind + dx + 1, :, :] = (pltpu.roll(value, (-dx) % LANES, 1) if dx else value) - 1.0


def one_hot(shift_ref, row):
    sub = lax.broadcasted_iota(jnp.int32, (8, LANES), 0)
    low = sub.astype(f32)
    high = low + 8.0
    mid = jnp.where(sub < 4, sub + 8, sub - 4).astype(f32)
    late = low + 4.0
    first4 = sub < 4

    def spread(kind, t):
        dy, dx = t // 3 - 1, t % 3
        return jnp.broadcast_to(shift_ref[3 * kind + dx, pl.ds(row + dy, 1), :], (8, LANES))

    tiles = []
    for t in range(9):
        value = spread(1, t)
        tiles += [value == low, value == high]
    soils = [spread(0, t) for t in range(9)]
    for t in range(0, 9, 2):
        after = soils[t + 1] if t < 8 else jnp.full((8, LANES), -9.0, f32)
        tiles += [soils[t] == low, jnp.where(first4, soils[t], after) == mid]
        if t < 8:
            tiles.append(after == late)
    pairs = [
        jnp.concatenate([jnp.where(a, 1.0, 0.0), jnp.where(b, 1.0, 0.0)], axis=0).astype(bf16)
        for a, b in zip(tiles[0::2], tiles[1::2])
    ]
    return jnp.concatenate(pairs, axis=0)


def conduct_rows(shift_ref, at, table, proj):
    hot = jnp.concatenate([one_hot(shift_ref, at), one_hot(shift_ref, at + 1)], axis=1)
    both = jnp.dot(table, hot, preferred_element_type=f32)
    hidden = jnp.maximum(both[:LANES] + both[LANES:], 0.0).astype(bf16)
    value = jnp.exp(jnp.dot(proj, hidden, preferred_element_type=f32))
    out = []
    for k in range(2):
        inside = jnp.broadcast_to(shift_ref[1, pl.ds(at + k, 1), :], (8, LANES)) >= 0.0
        out.append(jnp.where(inside, value[:, k * LANES : (k + 1) * LANES], 0.0))
    return out


def own_kernel(c_ref, table_ref, proj_ref, cond_ref, shift_ref):
    rows = c_ref.shape[1]
    for kind in range(2):
        shift_classes(shift_ref, kind, c_ref[5 + kind])
    table, proj = table_ref[...], proj_ref[...]

    def step(i, carry):
        for k, value in enumerate(conduct_rows(shift_ref, 2 * i + OWN, table, proj)):
            cond_ref[pl.ds(pl.multiple_of(8 * (2 * i + k), 8), 8), :] = value
        return carry

    lax.fori_loop(0, rows // 2 - OWN, step, 0, unroll=UNROLL_OWN)


def main_kernel(
    z_ref, c_ref, own_ref, a_ref, b_ref, table_ref, proj_ref, out_ref,
    top_ref, bot_ref, shift_ref, cond_ref, press_ref, press2_ref, stor_ref, coef_ref, rhs_ref, flat_ref, src_ref,
):
    odd = lax.axis_index("gx") % 2 == 1
    rows = z_ref.shape[2]
    full = rows + 2 * HALO
    top_ref[...] = jnp.where(odd, b_ref[...], a_ref[...])
    bot_ref[...] = jnp.where(odd, a_ref[...], b_ref[...])

    for j in range(2):
        at = 21 * HALO + j * CROWS
        value = jnp.concatenate([top_ref[at : at + CROWS, :], c_ref[5 + j], bot_ref[at : at + CROWS, :]], axis=0)
        shift_classes(shift_ref, j, value)

    for j in range(5):
        at = (16 + j) * HALO
        flat_ref[j, 0:HALO, :] = top_ref[at : at + HALO, :]
        flat_ref[j, HALO : HALO + rows, :] = c_ref[j]
        flat_ref[j, HALO + rows : full, :] = bot_ref[at : at + HALO, :]

    for ref in (press_ref, press2_ref):
        ref[0:8, :] = jnp.zeros((8, LANES), f32)
        ref[8 * (full + 1) :, :] = jnp.zeros((8, LANES), f32)
    for f, ref in ((0, press_ref), (1, stor_ref)):
        for r in range(0, full, 8):
            parts = []
            for l in range(8):
                k = 8 * f + l
                if r < HALO:
                    part = top_ref[k * HALO + r : k * HALO + r + 8, :]
                elif r < HALO + rows:
                    part = z_ref[l // 2, 2 * f + l % 2, r - HALO : r - HALO + 8, :]
                else:
                    at = k * HALO + r - HALO - rows
                    part = bot_ref[at : at + 8, :]
                parts.append(part)
            mixed = jnp.swapaxes(jnp.stack(parts), 0, 1).reshape(64, LANES)
            ref[8 * (r + 1) : 8 * (r + 9), :] = mixed

    table, proj = table_ref[...], proj_ref[...]
    cond_ref[8 * (HALO + OWN + 1) : 8 * (HALO + rows - OWN + 1), :] = own_ref[...]
    half = (HALO + OWN) // 2

    def step(i, carry):
        for row in (2 * i, full - 2 * half + 2 * i):
            for k, value in enumerate(conduct_rows(shift_ref, row + CROWS - HALO, table, proj)):
                cond_ref[at_row(row + k), :] = value
        return carry

    lax.fori_loop(0, half, step, 0, unroll=UNROLL_C)
    sub = lax.broadcasted_iota(jnp.int32, (8, LANES), 0)

    def row_coefficients(r):
        mid = cond_ref[at_row(r), :]
        north = 0.5 * lateral * (mid + cond_ref[at_row(r - 1), :])
        south = 0.5 * lateral * (mid + cond_ref[at_row(r + 1), :])
        east = 0.5 * lateral * (mid + pltpu.roll(mid, LANES - 1, 1))
        west = pltpu.roll(east, 1, 1)
        up = 0.5 * vertical * (mid + jnp.where(sub > 0, pltpu.roll(mid, 1, 0), 0.0))
        down = 0.5 * vertical * (mid + jnp.where(sub < 7, pltpu.roll(mid, 7, 0), 0.0))
        store = stor_ref[at_row(r), :]
        diagonal = store + up + down + north + south + east + west
        live = store > 0.0
        inverse = jnp.where(live, 1.0, 0.0) / jnp.where(live, diagonal, 1.0)
        here = at_row(r - 1)
        coef_ref[0, here, :] = jnp.where(sub > 0, up * inverse, 0.0)
        coef_ref[1, here, :] = jnp.where(sub < 7, down * inverse, 0.0)
        coef_ref[2, here, :] = north * inverse
        coef_ref[3, here, :] = south * inverse
        coef_ref[4, here, :] = east * inverse
        coef_ref[5, here, :] = west * inverse
        coef_ref[6, here, :] = store * inverse
        coef_ref[7, here, :] = jnp.where(sub == 0, inverse, 0.0)

    row_blocks(0, full, BLOCK_K, row_coefficients)
    for k in range(8):
        coef_ref[k, 0:8, :] = jnp.zeros((8, LANES), f32)
        coef_ref[k, 8 * (full - 1) : 8 * full, :] = jnp.zeros((8, LANES), f32)

    rough, rain, evap, elev = flat_ref[0], flat_ref[1], flat_ref[2], flat_ref[3]
    head = flat_ref[4]
    land = jnp.where(rough > 0.0, 1.0, 0.0)

    def around(value):
        return (
            pltpu.roll(value, full - 1, 0),
            pltpu.roll(value, 1, 0),
            pltpu.roll(value, LANES - 1, 1),
            pltpu.roll(value, 1, 1),
        )

    faces = [0.5 * (rough + near) for near in around(rough)]
    top_cond = cond_ref[pl.ds(8, full, stride=8), :]
    rate = land * (infil_rate * top_cond / (1.0 + top_cond))
    loss = land * evap
    for cycle in range(CYCLES):
        top = press_ref[pl.ds(8, full, stride=8), :]
        level = head + elev
        flux = jnp.zeros_like(level)
        for face, near in zip(faces, around(level)):
            flux = flux + face * (near - level)
        infil = rate * (head - top)
        src_ref[...] = infil - loss * jax.nn.sigmoid(top)
        head = head + land * (rain - infil + flux)
        done = cycle * SWEEPS

        for sweep in range(SWEEPS):
            old, new = (press_ref, press2_ref) if sweep % 2 == 0 else (press2_ref, press_ref)

            def one_row(r):
                here = at_row(r - 1)
                mid = old[at_row(r), :]
                if sweep == 0:
                    source = jnp.broadcast_to(src_ref[pl.ds(r, 1), :], (8, LANES))
                    rhs = coef_ref[6, here, :] * mid + coef_ref[7, here, :] * source
                    rhs_ref[here, :] = rhs
                else:
                    rhs = rhs_ref[here, :]
                column = coef_ref[0, here, :] * beside(old, mid, r, -1) + coef_ref[1, here, :] * beside(old, mid, r, 1)
                across = coef_ref[2, here, :] * old[at_row(r - 1), :] + coef_ref[3, here, :] * old[at_row(r + 1), :]
                along = coef_ref[4, here, :] * pltpu.roll(mid, LANES - 1, 1) + coef_ref[5, here, :] * pltpu.roll(mid, 1, 1)
                new[at_row(r), :] = (rhs + column) + (across + along)

            first = done + sweep + 1
            low = first // STEP_S * STEP_S
            row_blocks(low, full - low, (full - 2 * low) // TRIPS_S, one_row)

    lane = lax.broadcasted_iota(jnp.int32, (8, LANES), 1)
    for r in range(HALO, HALO + rows, 8):
        layers = jnp.swapaxes(press_ref[8 * (r + 1) : 8 * (r + 9), :].reshape(8, 8, LANES), 0, 1)
        for s in range(4):
            out_ref[s, 0, r - HALO : r - HALO + 8, :] = jnp.where(
                lane < CHUNK,
                pltpu.roll(layers[2 * s], LANES - EDGE, 1),
                pltpu.roll(layers[2 * s + 1], EDGE, 1),
            )
            out_ref[s, 1, r - HALO : r - HALO + 8, :] = pltpu.roll(head[r : r + 8], LANES - EDGE, 1)


def finish_kernel(z_ref, press_ref, head_ref):
    rows = z_ref.shape[2]
    lane = lax.broadcasted_iota(jnp.int32, (rows, LANES), 1)
    for d in range(0, 4, 2):
        cols = slice(d * CHUNK, d * CHUNK + LANES)
        a, b = z_ref[d, 0], z_ref[d + 1, 0]
        press_ref[0, :, cols] = jnp.where(lane < CHUNK, a, pltpu.roll(b, CHUNK, 1))
        press_ref[1, :, cols] = jnp.where(lane < CHUNK, pltpu.roll(a, CHUNK, 1), b)
        head_ref[:, cols] = jnp.where(lane < CHUNK, z_ref[d, 1], pltpu.roll(z_ref[d + 1, 1], CHUNK, 1))


def main_call(rows, args):
    full = rows + 2 * HALO
    grid = (8 * full, LANES)
    framed = (8 * (full + 2), LANES)
    return call(
        main_kernel, (jax.ShapeDtypeStruct((4, 2, rows, LANES), f32),), args,
        scratch=[
            pltpu.VMEM((MSG_ROWS, LANES), f32),
            pltpu.VMEM((MSG_ROWS, LANES), f32),
            pltpu.VMEM((6, rows + 2 * CROWS, LANES), f32),
            pltpu.VMEM(framed, f32),
            pltpu.VMEM(framed, f32),
            pltpu.VMEM(framed, f32),
            pltpu.VMEM(framed, f32),
            pltpu.VMEM((8,) + grid, f32),
            pltpu.VMEM(grid, f32),
            pltpu.VMEM((5, full, LANES), f32),
            pltpu.VMEM((full, LANES), f32),
        ],
        name="cycles",
    )[0]


def shards(
    soil_class, geology_class, land_mask, river_mask, elevation, roughness, rainfall, potential_evap,
    surface_head, pressure, storage, soil_embed, geology_embed, conv_weight, out_weight,
):
    rows, width = soil_class.shape
    n_gx, n_gy = lax.axis_size("gx"), lax.axis_size("gy")
    sds = jax.ShapeDtypeStruct
    raw = (
        soil_class, geology_class, land_mask, river_mask, elevation, roughness, rainfall,
        potential_evap, surface_head, pressure, storage,
    )
    given = tuple(range(len(raw)))

    edge = sds((rows, 2 * LANES), f32)
    ya, yb = call(pack_cols_kernel, (edge, edge), raw, name="pack_cols", hbm=given)
    ya = lax.ppermute(ya, "gy", swap_pairs(n_gy, 0))
    yb = lax.ppermute(yb, "gy", swap_pairs(n_gy, 1))

    sel, tap = table_layout()
    (table,) = call(
        table_kernel, (sds((2 * LANES, KROWS), bf16),),
        (
            jnp.asarray(sel), jnp.asarray(tap), soil_embed, geology_embed,
            conv_weight.reshape(9, LANES, LANES),
        ),
        name="table", hbm=range(5),
    )
    proj = out_weight.T
    ya, yb, table = lax.optimization_barrier((ya, yb, table))

    z, cols = call(
        slice_kernel, (sds((4, 4, rows, LANES), f32), sds((7, rows, LANES), f32)), (*raw, ya, yb),
        scratch=[pltpu.VMEM((4, 7, rows, LANES), f32)], name="slices", hbm=given,
    )
    z = lax.all_to_all(z, "sec", 0, 0)
    (own,) = call(
        own_kernel, (sds((8 * (rows - 2 * OWN), LANES), f32),), (cols, table, proj),
        scratch=[pltpu.VMEM((6, rows, LANES), f32)], name="own_conduct", hbm=(2,),
    )
    z, own = lax.optimization_barrier((z, own))

    msg = sds((MSG_ROWS, LANES), f32)
    xa, xb = call(pack_rows_kernel, (msg, msg), (z, cols), name="pack_rows")
    xa = lax.ppermute(xa, "gx", swap_pairs(n_gx, 1))
    xb = lax.ppermute(xb, "gx", swap_pairs(n_gx, 0))
    out = main_call(rows, (z, cols, own, xa, xb, table, proj))
    out = lax.all_to_all(out, "sec", 0, 0)
    return call(finish_kernel, (sds(pressure.shape, f32), sds((rows, width), f32)), (out,), name="finish", final=True)


def solution(mesh):
    flat = P("gx", "gy")
    deep = P("sec", "gx", "gy")
    in_specs = (flat,) * 9 + (deep, deep) + (P(),) * 4
    return jax.shard_map(shards, mesh=mesh, in_specs=in_specs, out_specs=(deep, flat), check_vma=False)
```

```python
import functools

import jax
import jax.numpy as jnp
import numpy as np
from jax import lax
from jax.experimental import pallas as pl
from jax.experimental.pallas import tpu as pltpu
from jax.sharding import PartitionSpec as P

SWEEPS = 4
CYCLES = 4
HALO = SWEEPS * CYCLES
LANES = 128
CHUNK = 64
EDGE = (LANES - CHUNK) // 2
CROWS = 24
NSOIL = 12
NGEO = 16
KSOIL = 9 * NGEO
KROWS = 256

infil_rate = 0.3
lateral = 1.0
vertical = 0.5

VMEM = pl.BlockSpec(memory_space=pltpu.VMEM)
f32 = jnp.float32
bf16 = jnp.bfloat16


def call(kernel, outs, args, scratch=(), name=None, hbm=(), final=False):
    made = outs if final else tuple(pltpu.VMEM(o.shape, o.dtype) for o in outs)
    args = [x if i in hbm else pltpu.with_memory_space_constraint(x, pltpu.VMEM) for i, x in enumerate(args)]
    return pl.pallas_call(
        kernel,
        out_shape=made,
        in_specs=[VMEM] * len(args),
        out_specs=tuple(VMEM for _ in outs),
        scratch_shapes=scratch,
        name=name,
    )(*args)


def swap_pairs(count, first):
    out = []
    for i in range(first, count - 1, 2):
        out += [(i, i + 1), (i + 1, i)]
    return out


def table_layout():
    sel = np.zeros((KROWS, NSOIL + NGEO), np.float32)
    tap = np.full((KROWS, LANES), -1, np.int32)
    for k in range(KSOIL):
        sel[k, NSOIL + k % NGEO] = 1
        tap[k] = k // NGEO
    for j in range(9 * NSOIL):
        sel[KSOIL + j, j % NSOIL] = 1
        tap[KSOIL + j] = j // NSOIL
    return sel, tap


def table_kernel(sel_ref, tap_ref, soil_ref, geo_ref, weight_ref, table_ref):
    sel = sel_ref[...].astype(bf16)
    embed = jnp.dot(sel[:, :NSOIL], soil_ref[...], preferred_element_type=f32)
    embed = embed + jnp.dot(sel[:, NSOIL:], geo_ref[...], preferred_element_type=f32)
    tap = tap_ref[...]
    total = jnp.zeros((LANES, KROWS), f32)
    for t in range(9):
        mine = jnp.where(tap == t, embed, 0.0).astype(bf16)
        total = total + lax.dot_general(
            weight_ref[t], mine, (((0,), (1,)), ((), ())), preferred_element_type=f32
        )
    high = total.astype(bf16)
    table_ref[0:LANES, :] = high
    table_ref[LANES : 2 * LANES, :] = (total - high.astype(f32)).astype(bf16)


def columns(soil, geo, land, river, elev, rough, rain, evap, head):
    landf = land.astype(f32)
    conveyance = landf * (1.0 + river.astype(f32)) * rough
    return (
        [conveyance, rain, evap, elev, head],
        [(soil + 1).astype(f32), (geo + 1).astype(f32)],
    )


def pack_cols_kernel(
    soil, geo, land, river, elev, rough, rain, evap, head, press, stor, a_ref, b_ref
):
    odd = lax.axis_index("gy") % 2 == 1
    plain, classes = columns(
        soil[...], geo[...], land[...], river[...], elev[...], rough[...], rain[...], evap[...], head[...]
    )
    plain = [press[0], press[1], stor[0], stor[1]] + plain
    width = plain[0].shape[1]
    lane = lax.broadcasted_iota(jnp.int32, (plain[0].shape[0], LANES), 1)

    def side(right):
        halves = []
        for half in range(2):
            acc = jnp.zeros((plain[0].shape[0], LANES), f32)
            items = []
            if half == 0:
                items = [(plain[i], 16, 16 * i) for i in range(8)]
            else:
                items = [(plain[8], 16, 0), (classes[0], 32, 32), (classes[1], 32, 64)]
            for value, wide, at in items:
                part = value[:, width - LANES :] if right else value[:, :LANES]
                start = LANES - wide if right else 0
                moved = part if start == at else pltpu.roll(part, (at - start) % LANES, 1)
                acc = jnp.where((lane >= at) & (lane < at + wide), moved, acc)
            halves.append(acc)
        return halves

    left, right = side(False), side(True)
    for half in range(2):
        cols = slice(half * LANES, (half + 1) * LANES)
        a_ref[:, cols] = jnp.where(odd, left[half], right[half])
        b_ref[:, cols] = jnp.where(odd, right[half], left[half])


def slice_kernel(
    soil, geo, land, river, elev, rough, rain, evap, head, press, stor, a_ref, b_ref,
    z_ref, c_ref, ca_ref, cb_ref, work_ref,
):
    odd = lax.axis_index("gy") % 2 == 1
    plain, classes = columns(
        soil[...], geo[...], land[...], river[...], elev[...], rough[...], rain[...], evap[...], head[...]
    )
    plain = [press[0], press[1], stor[0], stor[1]] + plain
    rows, width = plain[0].shape
    lane = lax.broadcasted_iota(jnp.int32, (rows, LANES), 1)
    got_a, got_b = a_ref[...], b_ref[...]
    left = jnp.where(odd, got_a, got_b)
    right = jnp.where(odd, got_b, got_a)

    def slices(value, half, at, wide):
        cols = slice(half * LANES, (half + 1) * LANES)
        lo, hi = left[:, cols], right[:, cols]
        move = (EDGE - wide - at) % LANES
        lo = pltpu.roll(lo, move, 1) if move else lo
        move = (LANES - EDGE - at) % LANES
        hi = pltpu.roll(hi, move, 1) if move else hi
        first, last = value[:, :LANES], value[:, width - LANES :]
        low_r, high_r = pltpu.roll(first, EDGE, 1), pltpu.roll(last, EDGE, 1)
        low_l, high_l = pltpu.roll(first, LANES - EDGE, 1), pltpu.roll(last, LANES - EDGE, 1)
        zero = jnp.zeros_like(lo)
        return [
            jnp.where(lane < EDGE, jnp.where(lane >= EDGE - wide, lo, zero), low_r),
            jnp.where(lane < LANES - EDGE, low_l, high_l),
            jnp.where(lane < EDGE, low_r, high_r),
            jnp.where(lane < LANES - EDGE, high_l, jnp.where(lane < LANES - EDGE + wide, hi, zero)),
        ]

    for i in range(4):
        for d, part in enumerate(slices(plain[i], 0, 16 * i, 16)):
            z_ref[d, i] = part
    spots = [(0, 16 * i, 16) for i in range(4, 8)] + [(1, 0, 16), (1, 32, 32), (1, 64, 32)]
    for j, (value, (half, at, wide)) in enumerate(zip(plain[4:] + classes, spots)):
        for d, part in enumerate(slices(value, half, at, wide)):
            work_ref[d, j] = part
    c_ref[...] = work_ref[lax.axis_index("sec")]
    odd_x = lax.axis_index("gx") % 2 == 1
    low = jnp.where(odd_x, rows - HALO, 0)
    low_class = jnp.where(odd_x, rows - CROWS, 0)
    for ref, at, at_class in (
        (ca_ref, low, low_class),
        (cb_ref, (rows - HALO) - low, (rows - CROWS) - low_class),
    ):
        for j in range(5):
            ref[j * HALO : (j + 1) * HALO, :] = c_ref[j, pl.ds(pl.multiple_of(at, 8), HALO), :]
        for j in range(2):
            to = 5 * HALO + j * CROWS
            ref[to : to + CROWS, :] = c_ref[5 + j, pl.ds(pl.multiple_of(at_class, 8), CROWS), :]


def pack_rows_kernel(z_ref, a_ref, b_ref):
    odd = lax.axis_index("gx") % 2 == 1
    rows = z_ref.shape[2]
    low = jnp.where(odd, rows - HALO, 0)
    lane = lax.broadcasted_iota(jnp.int32, (HALO, LANES), 1)
    free = (lane < EDGE - HALO) | (lane >= LANES - EDGE + HALO)
    for ref, at in ((a_ref, low), (b_ref, (rows - HALO) - low)):
        at = pl.multiple_of(at, 8)
        for s in range(4):
            last = z_ref[s, 3, pl.ds(at, HALO), :]
            for i in range(3):
                k = (3 * s + i) * HALO
                moved = pltpu.roll(last, LANES - EDGE * (i + 1), 1)
                ref[k : k + HALO, :] = jnp.where(free, moved, z_ref[s, i, pl.ds(at, HALO), :])


def unpack(ref, s):
    lane = lax.broadcasted_iota(jnp.int32, (HALO, LANES), 1)
    parts = [ref[(3 * s + i) * HALO : (3 * s + i + 1) * HALO, :] for i in range(3)]
    last = jnp.zeros((HALO, LANES), f32)
    for i, part in enumerate(parts):
        start = EDGE - HALO + EDGE * i
        last = jnp.where((lane >= start) & (lane < start + EDGE), pltpu.roll(part, EDGE * (i + 1), 1), last)
    return parts + [last]


MSG_ROWS = 12 * HALO
MSG_ROWS_2D = 5 * HALO + 2 * CROWS


STEP_S = 8
TRIPS_S = 1
BLOCK_K = 16
UNROLL_C = 8


def at_row(r):
    return pl.ds(pl.multiple_of(8 * r + 8, 8), 8)


def place(ref, r):
    return ref.at[at_row(r), :]


def beside(ref, mid, r, step):
    return pltpu.roll(mid, (-step) % 8, 0)


def row_blocks(low, high, size, body):
    assert (high - low) % size == 0

    def step(b, carry):
        for i in range(size):
            body(low + b * size + i)
        return carry

    lax.fori_loop(0, (high - low) // size, step, 0)


def shift_classes(ref, kind, value):
    for dx in (-1, 0, 1):
        ref[3 * kind + dx + 1, :, :] = (pltpu.roll(value, (-dx) % LANES, 1) if dx else value) - 1.0


def one_hot(shift_ref, row):
    sub = lax.broadcasted_iota(jnp.int32, (8, LANES), 0)
    low = sub.astype(f32)
    high = low + 8.0
    mid = jnp.where(sub < 4, sub + 8, sub - 4).astype(f32)
    late = low + 4.0
    first4 = sub < 4

    def spread(kind, t):
        dy, dx = t // 3 - 1, t % 3
        return jnp.broadcast_to(shift_ref[3 * kind + dx, pl.ds(row + dy, 1), :], (8, LANES))

    tiles = []
    for t in range(9):
        value = spread(1, t)
        tiles += [value == low, value == high]
    soils = [spread(0, t) for t in range(9)]
    for t in range(0, 9, 2):
        after = soils[t + 1] if t < 8 else jnp.full((8, LANES), -9.0, f32)
        tiles += [soils[t] == low, jnp.where(first4, soils[t], after) == mid]
        if t < 8:
            tiles.append(after == late)
    pairs = [
        jnp.concatenate([jnp.where(a, 1.0, 0.0), jnp.where(b, 1.0, 0.0)], axis=0).astype(bf16)
        for a, b in zip(tiles[0::2], tiles[1::2])
    ]
    return jnp.concatenate(pairs, axis=0)


def conduct_rows(shift_ref, at, table, proj):
    hot = jnp.concatenate([one_hot(shift_ref, at), one_hot(shift_ref, at + 1)], axis=1)
    both = jnp.dot(table, hot, preferred_element_type=f32)
    hidden = jnp.maximum(both[:LANES] + both[LANES:], 0.0).astype(bf16)
    value = jnp.exp(jnp.dot(proj, hidden, preferred_element_type=f32))
    out = []
    for k in range(2):
        inside = jnp.broadcast_to(shift_ref[1, pl.ds(at + k, 1), :], (8, LANES)) >= 0.0
        out.append(jnp.where(inside, value[:, k * LANES : (k + 1) * LANES], 0.0))
    return out


def by_side(a_ref, b_ref):
    odd = lax.axis_index("gx") % 2 == 1
    a, b = a_ref[...], b_ref[...]
    return jnp.where(odd, b, a), jnp.where(odd, a, b)


def conduct_kernel(c_ref, ca_ref, cb_ref, table_ref, proj_ref, cond_ref, shift_ref):
    full = c_ref.shape[1] + 2 * HALO
    above, below = by_side(ca_ref, cb_ref)
    for kind in range(2):
        at = 5 * HALO + kind * CROWS
        value = jnp.concatenate([above[at : at + CROWS], c_ref[5 + kind], below[at : at + CROWS]], axis=0)
        shift_classes(shift_ref, kind, value)
    table, proj = table_ref[...], proj_ref[...]

    def step(i, carry):
        for k, value in enumerate(conduct_rows(shift_ref, 2 * i + CROWS - HALO, table, proj)):
            cond_ref[at_row(2 * i + k), :] = value
        return carry

    lax.fori_loop(0, full // 2, step, 0, unroll=UNROLL_C)
    cond_ref[0:8, :] = jnp.zeros((8, LANES), f32)
    cond_ref[8 * (full + 1) :, :] = jnp.zeros((8, LANES), f32)


def main_kernel(
    z_ref, c_ref, ca_ref, cb_ref, a_ref, b_ref, cond_ref, out_ref,
    press_ref, press2_ref, stor_ref, coef_ref, rhs_ref, flat_ref, src_ref,
):
    rows = z_ref.shape[2]
    full = rows + 2 * HALO
    above, below = by_side(ca_ref, cb_ref)

    for j in range(5):
        at = j * HALO
        flat_ref[j, 0:HALO, :] = above[at : at + HALO]
        flat_ref[j, HALO : HALO + rows, :] = c_ref[j]
        flat_ref[j, HALO + rows : full, :] = below[at : at + HALO]

    for ref in (press_ref, press2_ref):
        ref[0:8, :] = jnp.zeros((8, LANES), f32)
        ref[8 * (full + 1) :, :] = jnp.zeros((8, LANES), f32)
    north, south = by_side(a_ref, b_ref)
    sides = [[unpack(side, s) for s in range(4)] for side in (north, south)]
    for f, ref in ((0, press_ref), (1, stor_ref)):
        for r in range(0, full, 8):
            parts = []
            for l in range(8):
                s, i = l // 2, 2 * f + l % 2
                if r < HALO:
                    part = sides[0][s][i][r : r + 8]
                elif r < HALO + rows:
                    part = z_ref[s, i, r - HALO : r - HALO + 8, :]
                else:
                    at = r - HALO - rows
                    part = sides[1][s][i][at : at + 8]
                parts.append(part)
            mixed = jnp.swapaxes(jnp.stack(parts), 0, 1).reshape(64, LANES)
            ref[8 * (r + 1) : 8 * (r + 9), :] = mixed
    sub = lax.broadcasted_iota(jnp.int32, (8, LANES), 0)

    def row_coefficients(r):
        mid = cond_ref[at_row(r), :]
        north = 0.5 * lateral * (mid + cond_ref[at_row(r - 1), :])
        south = 0.5 * lateral * (mid + cond_ref[at_row(r + 1), :])
        east = 0.5 * lateral * (mid + pltpu.roll(mid, LANES - 1, 1))
        west = pltpu.roll(east, 1, 1)
        up = 0.5 * vertical * (mid + jnp.where(sub > 0, pltpu.roll(mid, 1, 0), 0.0))
        down = 0.5 * vertical * (mid + jnp.where(sub < 7, pltpu.roll(mid, 7, 0), 0.0))
        store = stor_ref[at_row(r), :]
        diagonal = store + up + down + north + south + east + west
        live = store > 0.0
        inverse = jnp.where(live, 1.0, 0.0) / jnp.where(live, diagonal, 1.0)
        here = at_row(r - 1)
        coef_ref[0, here, :] = jnp.where(sub > 0, up * inverse, 0.0)
        coef_ref[1, here, :] = jnp.where(sub < 7, down * inverse, 0.0)
        coef_ref[2, here, :] = north * inverse
        coef_ref[3, here, :] = south * inverse
        coef_ref[4, here, :] = east * inverse
        coef_ref[5, here, :] = west * inverse
        coef_ref[6, here, :] = store * inverse
        coef_ref[7, here, :] = jnp.where(sub == 0, inverse, 0.0)

    row_blocks(0, full, BLOCK_K, row_coefficients)
    for k in range(8):
        coef_ref[k, 0:8, :] = jnp.zeros((8, LANES), f32)
        coef_ref[k, 8 * (full - 1) : 8 * full, :] = jnp.zeros((8, LANES), f32)

    rough, rain, evap, elev = flat_ref[0], flat_ref[1], flat_ref[2], flat_ref[3]
    head = flat_ref[4]
    land = jnp.where(rough > 0.0, 1.0, 0.0)

    def around(value):
        return (
            pltpu.roll(value, full - 1, 0),
            pltpu.roll(value, 1, 0),
            pltpu.roll(value, LANES - 1, 1),
            pltpu.roll(value, 1, 1),
        )

    faces = [0.5 * (rough + near) for near in around(rough)]
    top_cond = cond_ref[pl.ds(8, full, stride=8), :]
    rate = land * (infil_rate * top_cond / (1.0 + top_cond))
    loss = land * evap
    for cycle in range(CYCLES):
        top = press_ref[pl.ds(8, full, stride=8), :]
        level = head + elev
        flux = jnp.zeros_like(level)
        for face, near in zip(faces, around(level)):
            flux = flux + face * (near - level)
        infil = rate * (head - top)
        src_ref[...] = infil - loss * jax.nn.sigmoid(top)
        head = head + land * (rain - infil + flux)
        done = cycle * SWEEPS

        for sweep in range(SWEEPS):
            old, new = (press_ref, press2_ref) if sweep % 2 == 0 else (press2_ref, press_ref)

            def one_row(r):
                here = at_row(r - 1)
                mid = old[at_row(r), :]
                if sweep == 0:
                    source = jnp.broadcast_to(src_ref[pl.ds(r, 1), :], (8, LANES))
                    rhs = coef_ref[6, here, :] * mid + coef_ref[7, here, :] * source
                    rhs_ref[here, :] = rhs
                else:
                    rhs = rhs_ref[here, :]
                column = coef_ref[0, here, :] * beside(old, mid, r, -1) + coef_ref[1, here, :] * beside(old, mid, r, 1)
                across = coef_ref[2, here, :] * old[at_row(r - 1), :] + coef_ref[3, here, :] * old[at_row(r + 1), :]
                along = coef_ref[4, here, :] * pltpu.roll(mid, LANES - 1, 1) + coef_ref[5, here, :] * pltpu.roll(mid, 1, 1)
                new[at_row(r), :] = (rhs + column) + (across + along)

            first = done + sweep + 1
            low = first // STEP_S * STEP_S
            row_blocks(low, full - low, (full - 2 * low) // TRIPS_S, one_row)

    lane = lax.broadcasted_iota(jnp.int32, (8, LANES), 1)
    for r in range(HALO, HALO + rows, 8):
        layers = jnp.swapaxes(press_ref[8 * (r + 1) : 8 * (r + 9), :].reshape(8, 8, LANES), 0, 1)
        for s in range(4):
            out_ref[s, 0, r - HALO : r - HALO + 8, :] = jnp.where(
                lane < CHUNK,
                pltpu.roll(layers[2 * s], LANES - EDGE, 1),
                pltpu.roll(layers[2 * s + 1], EDGE, 1),
            )
            out_ref[s, 1, r - HALO : r - HALO + 8, :] = pltpu.roll(head[r : r + 8], LANES - EDGE, 1)


def finish_kernel(z_ref, press_ref, head_ref):
    rows = z_ref.shape[2]
    lane = lax.broadcasted_iota(jnp.int32, (rows, LANES), 1)
    for d in range(0, 4, 2):
        cols = slice(d * CHUNK, d * CHUNK + LANES)
        a, b = z_ref[d, 0], z_ref[d + 1, 0]
        press_ref[0, :, cols] = jnp.where(lane < CHUNK, a, pltpu.roll(b, CHUNK, 1))
        press_ref[1, :, cols] = jnp.where(lane < CHUNK, pltpu.roll(a, CHUNK, 1), b)
        head_ref[:, cols] = jnp.where(lane < CHUNK, z_ref[d, 1], pltpu.roll(z_ref[d + 1, 1], CHUNK, 1))


def main_call(rows, args):
    full = rows + 2 * HALO
    grid = (8 * full, LANES)
    framed = (8 * (full + 2), LANES)
    return call(
        main_kernel, (jax.ShapeDtypeStruct((4, 2, rows, LANES), f32),), args,
        scratch=[
            pltpu.VMEM(framed, f32),
            pltpu.VMEM(framed, f32),
            pltpu.VMEM(framed, f32),
            pltpu.VMEM((8,) + grid, f32),
            pltpu.VMEM(grid, f32),
            pltpu.VMEM((5, full, LANES), f32),
            pltpu.VMEM((full, LANES), f32),
        ],
        name="cycles",
    )[0]


def shards(
    soil_class, geology_class, land_mask, river_mask, elevation, roughness, rainfall, potential_evap,
    surface_head, pressure, storage, soil_embed, geology_embed, conv_weight, out_weight,
):
    rows, width = soil_class.shape
    n_gx, n_gy = lax.axis_size("gx"), lax.axis_size("gy")
    sds = jax.ShapeDtypeStruct
    raw = (
        soil_class, geology_class, land_mask, river_mask, elevation, roughness, rainfall,
        potential_evap, surface_head, pressure, storage,
    )
    given = tuple(range(len(raw)))

    edge = sds((rows, 2 * LANES), f32)
    ya, yb = call(pack_cols_kernel, (edge, edge), raw, name="pack_cols", hbm=given)
    ya = lax.ppermute(ya, "gy", swap_pairs(n_gy, 0))
    yb = lax.ppermute(yb, "gy", swap_pairs(n_gy, 1))

    plane, edge_2d = sds((7, rows, LANES), f32), sds((MSG_ROWS_2D, LANES), f32)
    z, cols, ca, cb = call(
        slice_kernel, (sds((4, 4, rows, LANES), f32), plane, edge_2d, edge_2d), (*raw, ya, yb),
        scratch=[pltpu.VMEM((4, 7, rows, LANES), f32)], name="slices", hbm=given,
    )
    z = lax.all_to_all(z, "sec", 0, 0)

    ca = lax.ppermute(ca, "gx", swap_pairs(n_gx, 1))
    cb = lax.ppermute(cb, "gx", swap_pairs(n_gx, 0))
    cols, soil_embed = lax.optimization_barrier((cols, soil_embed))
    sel, tap = table_layout()
    (table,) = call(
        table_kernel, (sds((2 * LANES, KROWS), bf16),),
        (
            jnp.asarray(sel), jnp.asarray(tap), soil_embed, geology_embed,
            conv_weight.reshape(9, LANES, LANES),
        ),
        name="table", hbm=range(5),
    )
    z, ca, cb, table = lax.optimization_barrier((z, ca, cb, table))

    msg = sds((MSG_ROWS, LANES), f32)
    xa, xb = call(pack_rows_kernel, (msg, msg), (z,), name="pack_rows")
    xa, xb, cols = lax.optimization_barrier((xa, xb, cols))
    xa = lax.ppermute(xa, "gx", swap_pairs(n_gx, 1))
    xb = lax.ppermute(xb, "gx", swap_pairs(n_gx, 0))
    (cond,) = call(
        conduct_kernel, (sds((8 * (rows + 2 * HALO + 2), LANES), f32),), (cols, ca, cb, table, out_weight.T),
        scratch=[pltpu.VMEM((6, rows + 2 * CROWS, LANES), f32)], name="conduct", hbm=(4,),
    )
    xa, xb, cond = lax.optimization_barrier((xa, xb, cond))
    out = main_call(rows, (z, cols, ca, cb, xa, xb, cond))
    out = lax.all_to_all(out, "sec", 0, 0)
    return call(finish_kernel, (sds(pressure.shape, f32), sds((rows, width), f32)), (out,), name="finish", final=True)


def solution(mesh):
    flat = P("gx", "gy")
    deep = P("sec", "gx", "gy")
    in_specs = (flat,) * 9 + (deep, deep) + (P(),) * 4
    return jax.shard_map(shards, mesh=mesh, in_specs=in_specs, out_specs=(deep, flat), check_vma=False)
```

```python
import functools

import jax
import jax.numpy as jnp
import numpy as np
from jax import lax
from jax.experimental import pallas as pl
from jax.experimental.pallas import tpu as pltpu
from jax.sharding import PartitionSpec as P

SWEEPS = 4
CYCLES = 4
HALO = SWEEPS * CYCLES
LANES = 128
CHUNK = 64
EDGE = (LANES - CHUNK) // 2
CROWS = 24
NSOIL = 12
NGEO = 16
KSOIL = 9 * NGEO
KROWS = 256

infil_rate = 0.3
lateral = 1.0
vertical = 0.5

VMEM = pl.BlockSpec(memory_space=pltpu.VMEM)
f32 = jnp.float32
bf16 = jnp.bfloat16


def call(kernel, outs, args, scratch=(), name=None, hbm=(), final=False):
    made = outs if final else tuple(pltpu.VMEM(o.shape, o.dtype) for o in outs)
    args = [x if i in hbm else pltpu.with_memory_space_constraint(x, pltpu.VMEM) for i, x in enumerate(args)]
    return pl.pallas_call(
        kernel,
        out_shape=made,
        in_specs=[VMEM] * len(args),
        out_specs=tuple(VMEM for _ in outs),
        scratch_shapes=scratch,
        name=name,
    )(*args)


def swap_pairs(count, first):
    out = []
    for i in range(first, count - 1, 2):
        out += [(i, i + 1), (i + 1, i)]
    return out


def table_layout():
    sel = np.zeros((KROWS, NSOIL + NGEO), np.float32)
    tap = np.full((KROWS, LANES), -1, np.int32)
    for k in range(KSOIL):
        sel[k, NSOIL + k % NGEO] = 1
        tap[k] = k // NGEO
    for j in range(9 * NSOIL):
        sel[KSOIL + j, j % NSOIL] = 1
        tap[KSOIL + j] = j // NSOIL
    return sel, tap


def table_kernel(sel_ref, tap_ref, soil_ref, geo_ref, weight_ref, table_ref):
    sel = sel_ref[...].astype(bf16)
    embed = jnp.dot(sel[:, :NSOIL], soil_ref[...], preferred_element_type=f32)
    embed = embed + jnp.dot(sel[:, NSOIL:], geo_ref[...], preferred_element_type=f32)
    tap = tap_ref[...]
    total = jnp.zeros((LANES, KROWS), f32)
    for t in range(9):
        mine = jnp.where(tap == t, embed, 0.0).astype(bf16)
        total = total + lax.dot_general(
            weight_ref[t], mine, (((0,), (1,)), ((), ())), preferred_element_type=f32
        )
    high = total.astype(bf16)
    table_ref[0:LANES, :] = high
    table_ref[LANES : 2 * LANES, :] = (total - high.astype(f32)).astype(bf16)


def columns(soil, geo, land, river, elev, rough, rain, evap, head):
    landf = land.astype(f32)
    conveyance = landf * (1.0 + river.astype(f32)) * rough
    return (
        [conveyance, rain, evap, elev, head],
        [(soil + 1).astype(f32), (geo + 1).astype(f32)],
    )


def pack_cols_kernel(
    soil, geo, land, river, elev, rough, rain, evap, head, press, stor, a_ref, b_ref
):
    odd = lax.axis_index("gy") % 2 == 1
    plain, classes = columns(
        soil[...], geo[...], land[...], river[...], elev[...], rough[...], rain[...], evap[...], head[...]
    )
    plain = [press[0], press[1], stor[0], stor[1]] + plain
    width = plain[0].shape[1]
    lane = lax.broadcasted_iota(jnp.int32, (plain[0].shape[0], LANES), 1)

    def side(right):
        halves = []
        for half in range(2):
            acc = jnp.zeros((plain[0].shape[0], LANES), f32)
            items = []
            if half == 0:
                items = [(plain[i], 16, 16 * i) for i in range(8)]
            else:
                items = [(plain[8], 16, 0), (classes[0], 32, 32), (classes[1], 32, 64)]
            for value, wide, at in items:
                part = value[:, width - LANES :] if right else value[:, :LANES]
                start = LANES - wide if right else 0
                moved = part if start == at else pltpu.roll(part, (at - start) % LANES, 1)
                acc = jnp.where((lane >= at) & (lane < at + wide), moved, acc)
            halves.append(acc)
        return halves

    left, right = side(False), side(True)
    for half in range(2):
        cols = slice(half * LANES, (half + 1) * LANES)
        a_ref[:, cols] = jnp.where(odd, left[half], right[half])
        b_ref[:, cols] = jnp.where(odd, right[half], left[half])


def slice_kernel(
    soil, geo, land, river, elev, rough, rain, evap, head, press, stor, z_ref, c_ref, work_ref
):
    plain, classes = columns(
        soil[...], geo[...], land[...], river[...], elev[...], rough[...], rain[...], evap[...], head[...]
    )
    plain = [press[0], press[1], stor[0], stor[1]] + plain
    rows, width = plain[0].shape
    lane = lax.broadcasted_iota(jnp.int32, (rows, LANES), 1)

    def slices(value):
        first, last = value[:, :LANES], value[:, width - LANES :]
        low_r, high_r = pltpu.roll(first, EDGE, 1), pltpu.roll(last, EDGE, 1)
        low_l, high_l = pltpu.roll(first, LANES - EDGE, 1), pltpu.roll(last, LANES - EDGE, 1)
        return [
            jnp.where(lane < EDGE, 0.0, low_r),
            jnp.where(lane < LANES - EDGE, low_l, high_l),
            jnp.where(lane < EDGE, low_r, high_r),
            jnp.where(lane < LANES - EDGE, high_l, 0.0),
        ]

    for i in range(4):
        for d, part in enumerate(slices(plain[i])):
            z_ref[d, i] = part
    for j, value in enumerate(plain[4:] + classes):
        for d, part in enumerate(slices(value)):
            work_ref[d, j] = part
    c_ref[...] = work_ref[lax.axis_index("sec")]


def halo_kernel(z_in, c_in, a_ref, b_ref, z_ref, c_ref, ca_ref, cb_ref):
    odd = lax.axis_index("gy") % 2 == 1
    sec = lax.axis_index("sec")
    rows = c_in.shape[1]
    lane = lax.broadcasted_iota(jnp.int32, (rows, LANES), 1)
    got_a, got_b = a_ref[...], b_ref[...]
    left = jnp.where(odd, got_a, got_b)
    right = jnp.where(odd, got_b, got_a)

    def halos(half, at, wide):
        cols = slice(half * LANES, (half + 1) * LANES)
        lo, hi = left[:, cols], right[:, cols]
        move = (EDGE - wide - at) % LANES
        lo = pltpu.roll(lo, move, 1) if move else lo
        move = (LANES - EDGE - at) % LANES
        hi = pltpu.roll(hi, move, 1) if move else hi
        return (
            jnp.where((lane >= EDGE - wide) & (lane < EDGE), lo, 0.0),
            jnp.where((lane >= LANES - EDGE) & (lane < LANES - EDGE + wide), hi, 0.0),
        )

    inner_l, inner_r = lane >= EDGE, lane < LANES - EDGE
    for i in range(4):
        lo, hi = halos(0, 16 * i, 16)
        z_ref[0, i] = jnp.where(inner_l, z_in[0, i], lo)
        z_ref[1, i] = z_in[1, i]
        z_ref[2, i] = z_in[2, i]
        z_ref[3, i] = jnp.where(inner_r, z_in[3, i], hi)
    spots = [(0, 16 * i, 16) for i in range(4, 8)] + [(1, 0, 16), (1, 32, 32), (1, 64, 32)]
    for j, spot in enumerate(spots):
        lo, hi = halos(*spot)
        value = c_in[j]
        value = jnp.where(inner_l | (sec != 0), value, lo)
        c_ref[j] = jnp.where(inner_r | (sec != 3), value, hi)
    odd_x = lax.axis_index("gx") % 2 == 1
    low = jnp.where(odd_x, rows - HALO, 0)
    low_class = jnp.where(odd_x, rows - CROWS, 0)
    for ref, at, at_class in (
        (ca_ref, low, low_class),
        (cb_ref, (rows - HALO) - low, (rows - CROWS) - low_class),
    ):
        for j in range(5):
            ref[j * HALO : (j + 1) * HALO, :] = c_ref[j, pl.ds(pl.multiple_of(at, 8), HALO), :]
        for j in range(2):
            to = 5 * HALO + j * CROWS
            ref[to : to + CROWS, :] = c_ref[5 + j, pl.ds(pl.multiple_of(at_class, 8), CROWS), :]


def pack_rows_kernel(z_ref, a_ref, b_ref):
    odd = lax.axis_index("gx") % 2 == 1
    rows = z_ref.shape[2]
    low = jnp.where(odd, rows - HALO, 0)
    lane = lax.broadcasted_iota(jnp.int32, (HALO, LANES), 1)
    free = (lane < EDGE - HALO) | (lane >= LANES - EDGE + HALO)
    for ref, at in ((a_ref, low), (b_ref, (rows - HALO) - low)):
        at = pl.multiple_of(at, 8)
        for s in range(4):
            last = z_ref[s, 3, pl.ds(at, HALO), :]
            for i in range(3):
                k = (3 * s + i) * HALO
                moved = pltpu.roll(last, LANES - EDGE * (i + 1), 1)
                ref[k : k + HALO, :] = jnp.where(free, moved, z_ref[s, i, pl.ds(at, HALO), :])


def unpack(ref, s):
    lane = lax.broadcasted_iota(jnp.int32, (HALO, LANES), 1)
    parts = [ref[(3 * s + i) * HALO : (3 * s + i + 1) * HALO, :] for i in range(3)]
    last = jnp.zeros((HALO, LANES), f32)
    for i, part in enumerate(parts):
        start = EDGE - HALO + EDGE * i
        last = jnp.where((lane >= start) & (lane < start + EDGE), pltpu.roll(part, EDGE * (i + 1), 1), last)
    return parts + [last]


MSG_ROWS = 12 * HALO
MSG_ROWS_2D = 5 * HALO + 2 * CROWS


STEP_S = 8
TRIPS_S = 1
BLOCK_K = 16


def at_row(r):
    return pl.ds(pl.multiple_of(8 * r + 8, 8), 8)


def place(ref, r):
    return ref.at[at_row(r), :]


def beside(ref, mid, r, step):
    return pltpu.roll(mid, (-step) % 8, 0)


def row_blocks(low, high, size, body):
    assert (high - low) % size == 0

    def step(b, carry):
        for i in range(size):
            body(low + b * size + i)
        return carry

    lax.fori_loop(0, (high - low) // size, step, 0)


def shift_classes(ref, kind, value):
    for dx in (-1, 0, 1):
        ref[3 * kind + dx + 1, :, :] = (pltpu.roll(value, (-dx) % LANES, 1) if dx else value) - 1.0


def one_hot(shift_ref, row):
    sub = lax.broadcasted_iota(jnp.int32, (8, LANES), 0)
    low = sub.astype(f32)
    high = low + 8.0
    mid = jnp.where(sub < 4, sub + 8, sub - 4).astype(f32)
    late = low + 4.0
    first4 = sub < 4

    def spread(kind, t):
        dy, dx = t // 3 - 1, t % 3
        return jnp.broadcast_to(shift_ref[3 * kind + dx, pl.ds(row + dy, 1), :], (8, LANES))

    tiles = []
    for t in range(9):
        value = spread(1, t)
        tiles += [value == low, value == high]
    soils = [spread(0, t) for t in range(9)]
    for t in range(0, 9, 2):
        after = soils[t + 1] if t < 8 else jnp.full((8, LANES), -9.0, f32)
        tiles += [soils[t] == low, jnp.where(first4, soils[t], after) == mid]
        if t < 8:
            tiles.append(after == late)
    pairs = [
        jnp.concatenate([jnp.where(a, 1.0, 0.0), jnp.where(b, 1.0, 0.0)], axis=0).astype(bf16)
        for a, b in zip(tiles[0::2], tiles[1::2])
    ]
    return jnp.concatenate(pairs, axis=0)


def conduct_rows(shift_ref, at, count, table, proj):
    hot = jnp.concatenate([one_hot(shift_ref, at + k) for k in range(count)], axis=1)
    both = jnp.dot(table, hot, preferred_element_type=f32)
    hidden = jnp.maximum(both[:LANES] + both[LANES:], 0.0).astype(bf16)
    value = jnp.exp(jnp.dot(proj, hidden, preferred_element_type=f32))
    out = []
    for k in range(count):
        inside = jnp.broadcast_to(shift_ref[1, pl.ds(at + k, 1), :], (8, LANES)) >= 0.0
        out.append(jnp.where(inside, value[:, k * LANES : (k + 1) * LANES], 0.0))
    return out


def by_side(a_ref, b_ref):
    odd = lax.axis_index("gx") % 2 == 1
    a, b = a_ref[...], b_ref[...]
    return jnp.where(odd, b, a), jnp.where(odd, a, b)


def conduct_kernel(c_ref, ca_ref, cb_ref, table_ref, proj_ref, cond_ref, shift_ref):
    full = c_ref.shape[1] + 2 * HALO
    above, below = by_side(ca_ref, cb_ref)
    for kind in range(2):
        at = 5 * HALO + kind * CROWS
        value = jnp.concatenate([above[at : at + CROWS], c_ref[5 + kind], below[at : at + CROWS]], axis=0)
        shift_classes(shift_ref, kind, value)
    table, proj = table_ref[...], proj_ref[...]

    for row in range(0, full, full // 2):
        for k, value in enumerate(conduct_rows(shift_ref, row + CROWS - HALO, full // 2, table, proj)):
            cond_ref[at_row(row + k), :] = value
    cond_ref[0:8, :] = jnp.zeros((8, LANES), f32)
    cond_ref[8 * (full + 1) :, :] = jnp.zeros((8, LANES), f32)


def main_kernel(
    z_ref, c_ref, ca_ref, cb_ref, a_ref, b_ref, cond_ref, out_ref,
    press_ref, press2_ref, stor_ref, coef_ref, rhs_ref, flat_ref, src_ref,
):
    rows = z_ref.shape[2]
    full = rows + 2 * HALO
    above, below = by_side(ca_ref, cb_ref)

    for j in range(5):
        at = j * HALO
        flat_ref[j, 0:HALO, :] = above[at : at + HALO]
        flat_ref[j, HALO : HALO + rows, :] = c_ref[j]
        flat_ref[j, HALO + rows : full, :] = below[at : at + HALO]

    for ref in (press_ref, press2_ref):
        ref[0:8, :] = jnp.zeros((8, LANES), f32)
        ref[8 * (full + 1) :, :] = jnp.zeros((8, LANES), f32)
    north, south = by_side(a_ref, b_ref)
    sides = [[unpack(side, s) for s in range(4)] for side in (north, south)]
    for f, ref in ((0, press_ref), (1, stor_ref)):
        for r in range(0, full, 8):
            parts = []
            for l in range(8):
                s, i = l // 2, 2 * f + l % 2
                if r < HALO:
                    part = sides[0][s][i][r : r + 8]
                elif r < HALO + rows:
                    part = z_ref[s, i, r - HALO : r - HALO + 8, :]
                else:
                    at = r - HALO - rows
                    part = sides[1][s][i][at : at + 8]
                parts.append(part)
            mixed = jnp.swapaxes(jnp.stack(parts), 0, 1).reshape(64, LANES)
            ref[8 * (r + 1) : 8 * (r + 9), :] = mixed
    sub = lax.broadcasted_iota(jnp.int32, (8, LANES), 0)

    def row_coefficients(r):
        mid = cond_ref[at_row(r), :]
        north = 0.5 * lateral * (mid + cond_ref[at_row(r - 1), :])
        south = 0.5 * lateral * (mid + cond_ref[at_row(r + 1), :])
        east = 0.5 * lateral * (mid + pltpu.roll(mid, LANES - 1, 1))
        west = pltpu.roll(east, 1, 1)
        up = 0.5 * vertical * (mid + jnp.where(sub > 0, pltpu.roll(mid, 1, 0), 0.0))
        down = 0.5 * vertical * (mid + jnp.where(sub < 7, pltpu.roll(mid, 7, 0), 0.0))
        store = stor_ref[at_row(r), :]
        diagonal = store + up + down + north + south + east + west
        live = store > 0.0
        inverse = jnp.where(live, 1.0, 0.0) / jnp.where(live, diagonal, 1.0)
        here = at_row(r - 1)
        coef_ref[0, here, :] = jnp.where(sub > 0, up * inverse, 0.0)
        coef_ref[1, here, :] = jnp.where(sub < 7, down * inverse, 0.0)
        coef_ref[2, here, :] = north * inverse
        coef_ref[3, here, :] = south * inverse
        coef_ref[4, here, :] = east * inverse
        coef_ref[5, here, :] = west * inverse
        coef_ref[6, here, :] = store * inverse
        coef_ref[7, here, :] = jnp.where(sub == 0, inverse, 0.0)

    row_blocks(0, full, BLOCK_K, row_coefficients)
    for k in range(8):
        coef_ref[k, 0:8, :] = jnp.zeros((8, LANES), f32)
        coef_ref[k, 8 * (full - 1) : 8 * full, :] = jnp.zeros((8, LANES), f32)

    rough, rain, evap, elev = flat_ref[0], flat_ref[1], flat_ref[2], flat_ref[3]
    head = flat_ref[4]
    land = jnp.where(rough > 0.0, 1.0, 0.0)

    def around(value):
        return (
            pltpu.roll(value, full - 1, 0),
            pltpu.roll(value, 1, 0),
            pltpu.roll(value, LANES - 1, 1),
            pltpu.roll(value, 1, 1),
        )

    faces = [0.5 * (rough + near) for near in around(rough)]
    top_cond = cond_ref[pl.ds(8, full, stride=8), :]
    rate = land * (infil_rate * top_cond / (1.0 + top_cond))
    loss = land * evap
    for cycle in range(CYCLES):
        top = press_ref[pl.ds(8, full, stride=8), :]
        level = head + elev
        flux = jnp.zeros_like(level)
        for face, near in zip(faces, around(level)):
            flux = flux + face * (near - level)
        infil = rate * (head - top)
        src_ref[...] = infil - loss * jax.nn.sigmoid(top)
        head = head + land * (rain - infil + flux)
        done = cycle * SWEEPS

        for sweep in range(SWEEPS):
            old, new = (press_ref, press2_ref) if sweep % 2 == 0 else (press2_ref, press_ref)

            def one_row(r):
                here = at_row(r - 1)
                mid = old[at_row(r), :]
                if sweep == 0:
                    source = jnp.broadcast_to(src_ref[pl.ds(r, 1), :], (8, LANES))
                    rhs = coef_ref[6, here, :] * mid + coef_ref[7, here, :] * source
                    rhs_ref[here, :] = rhs
                else:
                    rhs = rhs_ref[here, :]
                column = coef_ref[0, here, :] * beside(old, mid, r, -1) + coef_ref[1, here, :] * beside(old, mid, r, 1)
                across = coef_ref[2, here, :] * old[at_row(r - 1), :] + coef_ref[3, here, :] * old[at_row(r + 1), :]
                along = coef_ref[4, here, :] * pltpu.roll(mid, LANES - 1, 1) + coef_ref[5, here, :] * pltpu.roll(mid, 1, 1)
                new[at_row(r), :] = (rhs + column) + (across + along)

            first = done + sweep + 1
            low = first // STEP_S * STEP_S
            row_blocks(low, full - low, (full - 2 * low) // TRIPS_S, one_row)

    lane = lax.broadcasted_iota(jnp.int32, (8, LANES), 1)
    for r in range(HALO, HALO + rows, 8):
        layers = jnp.swapaxes(press_ref[8 * (r + 1) : 8 * (r + 9), :].reshape(8, 8, LANES), 0, 1)
        for s in range(4):
            out_ref[s, 0, r - HALO : r - HALO + 8, :] = jnp.where(
                lane < CHUNK,
                pltpu.roll(layers[2 * s], LANES - EDGE, 1),
                pltpu.roll(layers[2 * s + 1], EDGE, 1),
            )
            out_ref[s, 1, r - HALO : r - HALO + 8, :] = pltpu.roll(head[r : r + 8], LANES - EDGE, 1)


def finish_kernel(z_ref, press_ref, head_ref):
    rows = z_ref.shape[2]
    lane = lax.broadcasted_iota(jnp.int32, (rows, LANES), 1)
    for d in range(0, 4, 2):
        cols = slice(d * CHUNK, d * CHUNK + LANES)
        a, b = z_ref[d, 0], z_ref[d + 1, 0]
        press_ref[0, :, cols] = jnp.where(lane < CHUNK, a, pltpu.roll(b, CHUNK, 1))
        press_ref[1, :, cols] = jnp.where(lane < CHUNK, pltpu.roll(a, CHUNK, 1), b)
        head_ref[:, cols] = jnp.where(lane < CHUNK, z_ref[d, 1], pltpu.roll(z_ref[d + 1, 1], CHUNK, 1))


def main_call(rows, args):
    full = rows + 2 * HALO
    grid = (8 * full, LANES)
    framed = (8 * (full + 2), LANES)
    return call(
        main_kernel, (jax.ShapeDtypeStruct((4, 2, rows, LANES), f32),), args,
        scratch=[
            pltpu.VMEM(framed, f32),
            pltpu.VMEM(framed, f32),
            pltpu.VMEM(framed, f32),
            pltpu.VMEM((8,) + grid, f32),
            pltpu.VMEM(grid, f32),
            pltpu.VMEM((5, full, LANES), f32),
            pltpu.VMEM((full, LANES), f32),
        ],
        name="cycles",
    )[0]


def shards(
    soil_class, geology_class, land_mask, river_mask, elevation, roughness, rainfall, potential_evap,
    surface_head, pressure, storage, soil_embed, geology_embed, conv_weight, out_weight,
):
    rows, width = soil_class.shape
    n_gx, n_gy = lax.axis_size("gx"), lax.axis_size("gy")
    sds = jax.ShapeDtypeStruct
    raw = (
        soil_class, geology_class, land_mask, river_mask, elevation, roughness, rainfall,
        potential_evap, surface_head, pressure, storage,
    )
    given = tuple(range(len(raw)))

    edge = sds((rows, 2 * LANES), f32)
    chunks, plane = sds((4, 4, rows, LANES), f32), sds((7, rows, LANES), f32)
    ya, yb = call(pack_cols_kernel, (edge, edge), raw, name="pack_cols", hbm=given)
    ya, yb, head = lax.optimization_barrier((ya, yb, surface_head))
    ya = lax.ppermute(ya, "gy", swap_pairs(n_gy, 0))
    yb = lax.ppermute(yb, "gy", swap_pairs(n_gy, 1))

    z, cols = call(
        slice_kernel, (chunks, plane), (*raw[:8], head, *raw[9:]),
        scratch=[pltpu.VMEM((4, 7, rows, LANES), f32)], name="slices", hbm=given,
    )
    ya, yb, z, cols = lax.optimization_barrier((ya, yb, z, cols))
    edge_2d = sds((MSG_ROWS_2D, LANES), f32)
    z, cols, ca, cb = call(
        halo_kernel, (chunks, plane, edge_2d, edge_2d), (z, cols, ya, yb), name="halo"
    )
    z = lax.all_to_all(z, "sec", 0, 0)

    ca = lax.ppermute(ca, "gx", swap_pairs(n_gx, 1))
    cb = lax.ppermute(cb, "gx", swap_pairs(n_gx, 0))
    z, ca, cb = lax.optimization_barrier((z, ca, cb))

    msg = sds((MSG_ROWS, LANES), f32)
    xa, xb = call(pack_rows_kernel, (msg, msg), (z,), name="pack_rows")
    xa, xb, cols, soil_embed = lax.optimization_barrier((xa, xb, cols, soil_embed))
    xa = lax.ppermute(xa, "gx", swap_pairs(n_gx, 1))
    xb = lax.ppermute(xb, "gx", swap_pairs(n_gx, 0))

    sel, tap = table_layout()
    (table,) = call(
        table_kernel, (sds((2 * LANES, KROWS), bf16),),
        (
            jnp.asarray(sel), jnp.asarray(tap), soil_embed, geology_embed,
            conv_weight.reshape(9, LANES, LANES),
        ),
        name="table", hbm=range(5),
    )
    (cond,) = call(
        conduct_kernel, (sds((8 * (rows + 2 * HALO + 2), LANES), f32),), (cols, ca, cb, table, out_weight.T),
        scratch=[pltpu.VMEM((6, rows + 2 * CROWS, LANES), f32)], name="conduct", hbm=(4,),
    )
    xa, xb, cond = lax.optimization_barrier((xa, xb, cond))
    out = main_call(rows, (z, cols, ca, cb, xa, xb, cond))
    out = lax.all_to_all(out, "sec", 0, 0)
    return call(finish_kernel, (sds(pressure.shape, f32), sds((rows, width), f32)), (out,), name="finish", final=True)


def solution(mesh):
    flat = P("gx", "gy")
    deep = P("sec", "gx", "gy")
    in_specs = (flat,) * 9 + (deep, deep) + (P(),) * 4
    return jax.shard_map(shards, mesh=mesh, in_specs=in_specs, out_specs=(deep, flat), check_vma=False)
```

```python
import jax
import jax.numpy as jnp
import numpy as np
from jax import lax
from jax.experimental import pallas as pl
from jax.experimental.pallas import tpu as pltpu
from jax.sharding import PartitionSpec as P


SWEEPS = 4
CYCLES = 4
HALO = SWEEPS * CYCLES
LANES = 128
CHUNK = 64
EDGE = (LANES - CHUNK) // 2
CROWS = 24
NSOIL = 12
NGEO = 16
KSOIL = 9 * NGEO
KROWS = 256

infil_rate = 0.3
lateral = 1.0
vertical = 0.5

VMEM = pl.BlockSpec(memory_space=pltpu.VMEM)
f32 = jnp.float32
bf16 = jnp.bfloat16


def call(kernel, outs, args, scratch=(), hbm=(), final=False):
    made = outs if final else tuple(pltpu.VMEM(o.shape, o.dtype) for o in outs)
    args = [x if i in hbm else pltpu.with_memory_space_constraint(x, pltpu.VMEM) for i, x in enumerate(args)]
    return pl.pallas_call(
        kernel, out_shape=made, in_specs=[VMEM] * len(args), out_specs=tuple(VMEM for _ in outs), scratch_shapes=scratch
    )(*args)


def swap_pairs(count, first):
    out = []
    for i in range(first, count - 1, 2):
        out += [(i, i + 1), (i + 1, i)]
    return out


def table_layout():
    sel = np.zeros((KROWS, NSOIL + NGEO), np.float32)
    tap = np.full((KROWS, LANES), -1, np.int32)
    for k in range(KSOIL):
        sel[k, NSOIL + k % NGEO] = 1
        tap[k] = k // NGEO
    for j in range(9 * NSOIL):
        sel[KSOIL + j, j % NSOIL] = 1
        tap[KSOIL + j] = j // NSOIL
    return sel, tap


def table_kernel(sel_ref, tap_ref, soil_ref, geo_ref, weight_ref, table_ref):
    sel = sel_ref[...].astype(bf16)
    embed = jnp.dot(sel[:, :NSOIL], soil_ref[...], preferred_element_type=f32)
    embed = embed + jnp.dot(sel[:, NSOIL:], geo_ref[...], preferred_element_type=f32)
    tap = tap_ref[...]
    total = jnp.zeros((LANES, KROWS), f32)
    for t in range(9):
        mine = jnp.where(tap == t, embed, 0.0).astype(bf16)
        total = total + lax.dot_general(
            weight_ref[t], mine, (((0,), (1,)), ((), ())), preferred_element_type=f32
        )
    high = total.astype(bf16)
    table_ref[0:LANES, :] = high
    table_ref[LANES : 2 * LANES, :] = (total - high.astype(f32)).astype(bf16)


def columns(soil, geo, land, river, elev, rough, rain, evap, head):
    landf = land.astype(f32)
    conveyance = landf * (1.0 + river.astype(f32)) * rough
    return (
        [conveyance, rain, evap, elev, head],
        [(soil + 1).astype(f32), (geo + 1).astype(f32)],
    )


def pack_cols_kernel(
    soil, geo, land, river, elev, rough, rain, evap, head, press, stor, a_ref, b_ref
):
    odd = lax.axis_index("gy") % 2 == 1
    plain, classes = columns(
        soil[...], geo[...], land[...], river[...], elev[...], rough[...], rain[...], evap[...], head[...]
    )
    plain = [press[0], press[1], stor[0], stor[1]] + plain
    width = plain[0].shape[1]
    lane = lax.broadcasted_iota(jnp.int32, (plain[0].shape[0], LANES), 1)

    def side(right):
        halves = []
        for half in range(2):
            acc = jnp.zeros((plain[0].shape[0], LANES), f32)
            items = []
            if half == 0:
                items = [(plain[i], 16, 16 * i) for i in range(8)]
            else:
                items = [(plain[8], 16, 0), (classes[0], 32, 32), (classes[1], 32, 64)]
            for value, wide, at in items:
                part = value[:, width - LANES :] if right else value[:, :LANES]
                start = LANES - wide if right else 0
                moved = part if start == at else pltpu.roll(part, (at - start) % LANES, 1)
                acc = jnp.where((lane >= at) & (lane < at + wide), moved, acc)
            halves.append(acc)
        return halves

    left, right = side(False), side(True)
    for half in range(2):
        cols = slice(half * LANES, (half + 1) * LANES)
        a_ref[:, cols] = jnp.where(odd, left[half], right[half])
        b_ref[:, cols] = jnp.where(odd, right[half], left[half])


def slice_kernel(
    soil, geo, land, river, elev, rough, rain, evap, head, press, stor, z_ref, c_ref, work_ref
):
    plain, classes = columns(
        soil[...], geo[...], land[...], river[...], elev[...], rough[...], rain[...], evap[...], head[...]
    )
    plain = [press[0], press[1], stor[0], stor[1]] + plain
    rows, width = plain[0].shape
    lane = lax.broadcasted_iota(jnp.int32, (rows, LANES), 1)

    def slices(value):
        first, last = value[:, :LANES], value[:, width - LANES :]
        low_r, high_r = pltpu.roll(first, EDGE, 1), pltpu.roll(last, EDGE, 1)
        low_l, high_l = pltpu.roll(first, LANES - EDGE, 1), pltpu.roll(last, LANES - EDGE, 1)
        return [
            jnp.where(lane < EDGE, 0.0, low_r),
            jnp.where(lane < LANES - EDGE, low_l, high_l),
            jnp.where(lane < EDGE, low_r, high_r),
            jnp.where(lane < LANES - EDGE, high_l, 0.0),
        ]

    for i in range(4):
        for d, part in enumerate(slices(plain[i])):
            z_ref[d, i] = part
    for j, value in enumerate(plain[4:] + classes):
        for d, part in enumerate(slices(value)):
            work_ref[d, j] = part
    c_ref[...] = work_ref[lax.axis_index("sec")]


def halo_kernel(z_in, c_in, a_ref, b_ref, z_ref, c_ref, ca_ref, cb_ref):
    odd = lax.axis_index("gy") % 2 == 1
    sec = lax.axis_index("sec")
    rows = c_in.shape[1]
    lane = lax.broadcasted_iota(jnp.int32, (rows, LANES), 1)
    got_a, got_b = a_ref[...], b_ref[...]
    left = jnp.where(odd, got_a, got_b)
    right = jnp.where(odd, got_b, got_a)

    def halos(half, at, wide):
        cols = slice(half * LANES, (half + 1) * LANES)
        lo, hi = left[:, cols], right[:, cols]
        move = (EDGE - wide - at) % LANES
        lo = pltpu.roll(lo, move, 1) if move else lo
        move = (LANES - EDGE - at) % LANES
        hi = pltpu.roll(hi, move, 1) if move else hi
        return (
            jnp.where((lane >= EDGE - wide) & (lane < EDGE), lo, 0.0),
            jnp.where((lane >= LANES - EDGE) & (lane < LANES - EDGE + wide), hi, 0.0),
        )

    inner_l, inner_r = lane >= EDGE, lane < LANES - EDGE
    for i in range(4):
        lo, hi = halos(0, 16 * i, 16)
        z_ref[0, i] = jnp.where(inner_l, z_in[0, i], lo)
        z_ref[1, i] = z_in[1, i]
        z_ref[2, i] = z_in[2, i]
        z_ref[3, i] = jnp.where(inner_r, z_in[3, i], hi)
    spots = [(0, 16 * i, 16) for i in range(4, 8)] + [(1, 0, 16), (1, 32, 32), (1, 64, 32)]
    for j, spot in enumerate(spots):
        lo, hi = halos(*spot)
        value = c_in[j]
        value = jnp.where(inner_l | (sec != 0), value, lo)
        c_ref[j] = jnp.where(inner_r | (sec != 3), value, hi)
    odd_x = lax.axis_index("gx") % 2 == 1
    low = jnp.where(odd_x, rows - HALO, 0)
    low_class = jnp.where(odd_x, rows - CROWS, 0)
    for ref, at, at_class in (
        (ca_ref, low, low_class),
        (cb_ref, (rows - HALO) - low, (rows - CROWS) - low_class),
    ):
        for j in range(5):
            ref[j * HALO : (j + 1) * HALO, :] = c_ref[j, pl.ds(pl.multiple_of(at, 8), HALO), :]
        for j in range(2):
            to = 5 * HALO + j * CROWS
            ref[to : to + CROWS, :] = c_ref[5 + j, pl.ds(pl.multiple_of(at_class, 8), CROWS), :]


def pack_rows_kernel(z_ref, a_ref, b_ref):
    odd = lax.axis_index("gx") % 2 == 1
    rows = z_ref.shape[2]
    low = jnp.where(odd, rows - HALO, 0)
    lane = lax.broadcasted_iota(jnp.int32, (HALO, LANES), 1)
    free = (lane < EDGE - HALO) | (lane >= LANES - EDGE + HALO)
    for ref, at in ((a_ref, low), (b_ref, (rows - HALO) - low)):
        at = pl.multiple_of(at, 8)
        for s in range(4):
            last = z_ref[s, 3, pl.ds(at, HALO), :]
            for i in range(3):
                k = (3 * s + i) * HALO
                moved = pltpu.roll(last, LANES - EDGE * (i + 1), 1)
                ref[k : k + HALO, :] = jnp.where(free, moved, z_ref[s, i, pl.ds(at, HALO), :])


def unpack(ref, s):
    lane = lax.broadcasted_iota(jnp.int32, (HALO, LANES), 1)
    parts = [ref[(3 * s + i) * HALO : (3 * s + i + 1) * HALO, :] for i in range(3)]
    last = jnp.zeros((HALO, LANES), f32)
    for i, part in enumerate(parts):
        start = EDGE - HALO + EDGE * i
        last = jnp.where((lane >= start) & (lane < start + EDGE), pltpu.roll(part, EDGE * (i + 1), 1), last)
    return parts + [last]


MSG_ROWS = 12 * HALO
MSG_ROWS_2D = 5 * HALO + 2 * CROWS


STEP_S = 8
TRIPS_S = 1
BLOCK_K = 16


def at_row(r):
    return pl.ds(pl.multiple_of(8 * r + 8, 8), 8)


def beside(mid, step):
    return pltpu.roll(mid, (-step) % 8, 0)


def row_blocks(low, high, size, body):
    assert (high - low) % size == 0

    def step(b, carry):
        for i in range(size):
            body(low + b * size + i)
        return carry

    lax.fori_loop(0, (high - low) // size, step, 0)


def shift_classes(ref, kind, value):
    for dx in (-1, 0, 1):
        ref[3 * kind + dx + 1, :, :] = (pltpu.roll(value, (-dx) % LANES, 1) if dx else value) - 1.0


def one_hot(shift_ref, row):
    sub = lax.broadcasted_iota(jnp.int32, (8, LANES), 0)
    low = sub.astype(f32)
    high = low + 8.0
    mid = jnp.where(sub < 4, sub + 8, sub - 4).astype(f32)
    late = low + 4.0
    first4 = sub < 4

    def spread(kind, t):
        dy, dx = t // 3 - 1, t % 3
        return jnp.broadcast_to(shift_ref[3 * kind + dx, pl.ds(row + dy, 1), :], (8, LANES))

    tiles = []
    for t in range(9):
        value = spread(1, t)
        tiles += [value == low, value == high]
    soils = [spread(0, t) for t in range(9)]
    for t in range(0, 9, 2):
        after = soils[t + 1] if t < 8 else jnp.full((8, LANES), -9.0, f32)
        tiles += [soils[t] == low, jnp.where(first4, soils[t], after) == mid]
        if t < 8:
            tiles.append(after == late)
    pairs = [
        jnp.concatenate([jnp.where(a, 1.0, 0.0), jnp.where(b, 1.0, 0.0)], axis=0).astype(bf16)
        for a, b in zip(tiles[0::2], tiles[1::2])
    ]
    return jnp.concatenate(pairs, axis=0)


def conduct_rows(shift_ref, at, count, table, proj):
    hot = jnp.concatenate([one_hot(shift_ref, at + k) for k in range(count)], axis=1)
    both = jnp.dot(table, hot, preferred_element_type=f32)
    hidden = jnp.maximum(both[:LANES] + both[LANES:], 0.0).astype(bf16)
    value = jnp.exp(jnp.dot(proj, hidden, preferred_element_type=f32))
    out = []
    for k in range(count):
        inside = jnp.broadcast_to(shift_ref[1, pl.ds(at + k, 1), :], (8, LANES)) >= 0.0
        out.append(jnp.where(inside, value[:, k * LANES : (k + 1) * LANES], 0.0))
    return out


def by_side(a_ref, b_ref):
    odd = lax.axis_index("gx") % 2 == 1
    a, b = a_ref[...], b_ref[...]
    return jnp.where(odd, b, a), jnp.where(odd, a, b)


def conduct_kernel(c_ref, ca_ref, cb_ref, table_ref, proj_ref, cond_ref, shift_ref):
    full = c_ref.shape[1] + 2 * HALO
    above, below = by_side(ca_ref, cb_ref)
    for kind in range(2):
        at = 5 * HALO + kind * CROWS
        value = jnp.concatenate([above[at : at + CROWS], c_ref[5 + kind], below[at : at + CROWS]], axis=0)
        shift_classes(shift_ref, kind, value)
    table, proj = table_ref[...], proj_ref[...]

    for row in range(0, full, full // 2):
        for k, value in enumerate(conduct_rows(shift_ref, row + CROWS - HALO, full // 2, table, proj)):
            cond_ref[at_row(row + k), :] = value
    cond_ref[0:8, :] = jnp.zeros((8, LANES), f32)
    cond_ref[8 * (full + 1) :, :] = jnp.zeros((8, LANES), f32)


def main_kernel(
    z_ref, c_ref, ca_ref, cb_ref, a_ref, b_ref, cond_ref, out_ref,
    press_ref, press2_ref, stor_ref, coef_ref, rhs_ref, flat_ref, src_ref,
):
    rows = z_ref.shape[2]
    full = rows + 2 * HALO
    above, below = by_side(ca_ref, cb_ref)

    for j in range(5):
        at = j * HALO
        flat_ref[j, 0:HALO, :] = above[at : at + HALO]
        flat_ref[j, HALO : HALO + rows, :] = c_ref[j]
        flat_ref[j, HALO + rows : full, :] = below[at : at + HALO]

    for ref in (press_ref, press2_ref):
        ref[0:8, :] = jnp.zeros((8, LANES), f32)
        ref[8 * (full + 1) :, :] = jnp.zeros((8, LANES), f32)
    north, south = by_side(a_ref, b_ref)
    sides = [[unpack(side, s) for s in range(4)] for side in (north, south)]
    for f, ref in ((0, press_ref), (1, stor_ref)):
        for r in range(0, full, 8):
            parts = []
            for l in range(8):
                s, i = l // 2, 2 * f + l % 2
                if r < HALO:
                    part = sides[0][s][i][r : r + 8]
                elif r < HALO + rows:
                    part = z_ref[s, i, r - HALO : r - HALO + 8, :]
                else:
                    at = r - HALO - rows
                    part = sides[1][s][i][at : at + 8]
                parts.append(part)
            mixed = jnp.swapaxes(jnp.stack(parts), 0, 1).reshape(64, LANES)
            ref[8 * (r + 1) : 8 * (r + 9), :] = mixed
    sub = lax.broadcasted_iota(jnp.int32, (8, LANES), 0)

    def row_coefficients(r):
        mid = cond_ref[at_row(r), :]
        north = 0.5 * lateral * (mid + cond_ref[at_row(r - 1), :])
        south = 0.5 * lateral * (mid + cond_ref[at_row(r + 1), :])
        east = 0.5 * lateral * (mid + pltpu.roll(mid, LANES - 1, 1))
        west = pltpu.roll(east, 1, 1)
        up = 0.5 * vertical * (mid + jnp.where(sub > 0, pltpu.roll(mid, 1, 0), 0.0))
        down = 0.5 * vertical * (mid + jnp.where(sub < 7, pltpu.roll(mid, 7, 0), 0.0))
        store = stor_ref[at_row(r), :]
        diagonal = store + up + down + north + south + east + west
        live = store > 0.0
        inverse = jnp.where(live, 1.0, 0.0) / jnp.where(live, diagonal, 1.0)
        here = at_row(r - 1)
        coef_ref[0, here, :] = jnp.where(sub > 0, up * inverse, 0.0)
        coef_ref[1, here, :] = jnp.where(sub < 7, down * inverse, 0.0)
        coef_ref[2, here, :] = north * inverse
        coef_ref[3, here, :] = south * inverse
        coef_ref[4, here, :] = east * inverse
        coef_ref[5, here, :] = west * inverse
        coef_ref[6, here, :] = store * inverse
        coef_ref[7, here, :] = jnp.where(sub == 0, inverse, 0.0)

    row_blocks(0, full, BLOCK_K, row_coefficients)
    for k in range(8):
        coef_ref[k, 0:8, :] = jnp.zeros((8, LANES), f32)
        coef_ref[k, 8 * (full - 1) : 8 * full, :] = jnp.zeros((8, LANES), f32)

    rough, rain, evap, elev = flat_ref[0], flat_ref[1], flat_ref[2], flat_ref[3]
    head = flat_ref[4]
    land = jnp.where(rough > 0.0, 1.0, 0.0)

    def around(value):
        return (
            pltpu.roll(value, full - 1, 0),
            pltpu.roll(value, 1, 0),
            pltpu.roll(value, LANES - 1, 1),
            pltpu.roll(value, 1, 1),
        )

    faces = [0.5 * (rough + near) for near in around(rough)]
    top_cond = cond_ref[pl.ds(8, full, stride=8), :]
    rate = land * (infil_rate * top_cond / (1.0 + top_cond))
    loss = land * evap
    for cycle in range(CYCLES):
        top = press_ref[pl.ds(8, full, stride=8), :]
        level = head + elev
        flux = jnp.zeros_like(level)
        for face, near in zip(faces, around(level)):
            flux = flux + face * (near - level)
        infil = rate * (head - top)
        src_ref[...] = infil - loss * jax.nn.sigmoid(top)
        head = head + land * (rain - infil + flux)
        done = cycle * SWEEPS

        for sweep in range(SWEEPS):
            old, new = (press_ref, press2_ref) if sweep % 2 == 0 else (press2_ref, press_ref)

            def one_row(r):
                here = at_row(r - 1)
                mid = old[at_row(r), :]
                if sweep == 0:
                    source = jnp.broadcast_to(src_ref[pl.ds(r, 1), :], (8, LANES))
                    rhs = coef_ref[6, here, :] * mid + coef_ref[7, here, :] * source
                    rhs_ref[here, :] = rhs
                else:
                    rhs = rhs_ref[here, :]
                column = coef_ref[0, here, :] * beside(mid, -1) + coef_ref[1, here, :] * beside(mid, 1)
                across = coef_ref[2, here, :] * old[at_row(r - 1), :] + coef_ref[3, here, :] * old[at_row(r + 1), :]
                along = coef_ref[4, here, :] * pltpu.roll(mid, LANES - 1, 1) + coef_ref[5, here, :] * pltpu.roll(mid, 1, 1)
                new[at_row(r), :] = (rhs + column) + (across + along)

            first = done + sweep + 1
            low = first // STEP_S * STEP_S
            row_blocks(low, full - low, (full - 2 * low) // TRIPS_S, one_row)

    lane = lax.broadcasted_iota(jnp.int32, (8, LANES), 1)
    for r in range(HALO, HALO + rows, 8):
        layers = jnp.swapaxes(press_ref[8 * (r + 1) : 8 * (r + 9), :].reshape(8, 8, LANES), 0, 1)
        for s in range(4):
            out_ref[s, 0, r - HALO : r - HALO + 8, :] = jnp.where(
                lane < CHUNK,
                pltpu.roll(layers[2 * s], LANES - EDGE, 1),
                pltpu.roll(layers[2 * s + 1], EDGE, 1),
            )
            out_ref[s, 1, r - HALO : r - HALO + 8, :] = pltpu.roll(head[r : r + 8], LANES - EDGE, 1)


def finish_kernel(z_ref, press_ref, head_ref):
    rows = z_ref.shape[2]
    lane = lax.broadcasted_iota(jnp.int32, (rows, LANES), 1)
    for d in range(0, 4, 2):
        cols = slice(d * CHUNK, d * CHUNK + LANES)
        a, b = z_ref[d, 0], z_ref[d + 1, 0]
        press_ref[0, :, cols] = jnp.where(lane < CHUNK, a, pltpu.roll(b, CHUNK, 1))
        press_ref[1, :, cols] = jnp.where(lane < CHUNK, pltpu.roll(a, CHUNK, 1), b)
        head_ref[:, cols] = jnp.where(lane < CHUNK, z_ref[d, 1], pltpu.roll(z_ref[d + 1, 1], CHUNK, 1))


def main_call(rows, args):
    full = rows + 2 * HALO
    grid = (8 * full, LANES)
    framed = (8 * (full + 2), LANES)
    return call(
        main_kernel, (jax.ShapeDtypeStruct((4, 2, rows, LANES), f32),), args,
        scratch=[
            pltpu.VMEM(framed, f32),
            pltpu.VMEM(framed, f32),
            pltpu.VMEM(framed, f32),
            pltpu.VMEM((8,) + grid, f32),
            pltpu.VMEM(grid, f32),
            pltpu.VMEM((5, full, LANES), f32),
            pltpu.VMEM((full, LANES), f32),
        ],
    )[0]


def shards(
    soil_class, geology_class, land_mask, river_mask, elevation, roughness, rainfall, potential_evap,
    surface_head, pressure, storage, soil_embed, geology_embed, conv_weight, out_weight,
):
    rows, width = soil_class.shape
    n_gx, n_gy = lax.axis_size("gx"), lax.axis_size("gy")
    sds = jax.ShapeDtypeStruct
    raw = (
        soil_class, geology_class, land_mask, river_mask, elevation, roughness, rainfall,
        potential_evap, surface_head, pressure, storage,
    )
    given = tuple(range(len(raw)))

    edge = sds((rows, 2 * LANES), f32)
    chunks, plane = sds((4, 4, rows, LANES), f32), sds((7, rows, LANES), f32)
    ya, yb = call(pack_cols_kernel, (edge, edge), raw, hbm=given)
    ya, yb, head = lax.optimization_barrier((ya, yb, surface_head))
    ya = lax.ppermute(ya, "gy", swap_pairs(n_gy, 0))
    yb = lax.ppermute(yb, "gy", swap_pairs(n_gy, 1))

    z, cols = call(
        slice_kernel, (chunks, plane), (*raw[:8], head, *raw[9:]),
        scratch=[pltpu.VMEM((4, 7, rows, LANES), f32)], hbm=given,
    )
    ya, yb, z, cols = lax.optimization_barrier((ya, yb, z, cols))
    edge_2d = sds((MSG_ROWS_2D, LANES), f32)
    z, cols, ca, cb = call(halo_kernel, (chunks, plane, edge_2d, edge_2d), (z, cols, ya, yb))
    z = lax.all_to_all(z, "sec", 0, 0)

    cb = lax.ppermute(cb, "gx", swap_pairs(n_gx, 0))
    ca = lax.ppermute(ca, "gx", swap_pairs(n_gx, 1))

    msg = sds((MSG_ROWS, LANES), f32)
    xa, xb = call(pack_rows_kernel, (msg, msg), (z,))
    xa, xb, cols, soil_embed = lax.optimization_barrier((xa, xb, cols, soil_embed))
    xa = lax.ppermute(xa, "gx", swap_pairs(n_gx, 1))
    xb = lax.ppermute(xb, "gx", swap_pairs(n_gx, 0))

    sel, tap = table_layout()
    (table,) = call(
        table_kernel, (sds((2 * LANES, KROWS), bf16),),
        (
            jnp.asarray(sel), jnp.asarray(tap), soil_embed, geology_embed,
            conv_weight.reshape(9, LANES, LANES),
        ),
        hbm=range(5),
    )
    (cond,) = call(
        conduct_kernel, (sds((8 * (rows + 2 * HALO + 2), LANES), f32),), (cols, ca, cb, table, out_weight.T),
        scratch=[pltpu.VMEM((6, rows + 2 * CROWS, LANES), f32)], hbm=(4,),
    )
    xa, xb, cond = lax.optimization_barrier((xa, xb, cond))
    out = main_call(rows, (z, cols, ca, cb, xa, xb, cond))
    out = lax.all_to_all(out, "sec", 0, 0)
    return call(finish_kernel, (sds(pressure.shape, f32), sds((rows, width), f32)), (out,), final=True)


def solution(mesh):
    flat = P("gx", "gy")
    deep = P("sec", "gx", "gy")
    in_specs = (flat,) * 9 + (deep, deep) + (P(),) * 4
    return jax.shard_map(shards, mesh=mesh, in_specs=in_specs, out_specs=(deep, flat), check_vma=False)
```

```python
import jax
import jax.numpy as jnp
import numpy as np
from jax import lax
from jax.experimental import pallas as pl
from jax.experimental.pallas import tpu as pltpu
from jax.sharding import PartitionSpec as P


SWEEPS = 4
CYCLES = 4
HALO = SWEEPS * CYCLES
LANES = 128
CHUNK = 64
EDGE = (LANES - CHUNK) // 2
CROWS = 24
NSOIL = 12
NGEO = 16
KSOIL = 9 * NGEO
KROWS = 256

infil_rate = 0.3
lateral = 1.0
vertical = 0.5

VMEM = pl.BlockSpec(memory_space=pltpu.VMEM)
f32 = jnp.float32
bf16 = jnp.bfloat16


def call(kernel, outs, args, scratch=(), hbm=(), final=False):
    made = outs if final else tuple(pltpu.VMEM(o.shape, o.dtype) for o in outs)
    args = [x if i in hbm else pltpu.with_memory_space_constraint(x, pltpu.VMEM) for i, x in enumerate(args)]
    return pl.pallas_call(
        kernel, out_shape=made, in_specs=[VMEM] * len(args), out_specs=tuple(VMEM for _ in outs), scratch_shapes=scratch
    )(*args)


def swap_pairs(count, first):
    out = []
    for i in range(first, count - 1, 2):
        out += [(i, i + 1), (i + 1, i)]
    return out


def table_layout():
    sel = np.zeros((KROWS, NSOIL + NGEO), np.float32)
    tap = np.full((KROWS, LANES), -1, np.int32)
    for k in range(KSOIL):
        sel[k, NSOIL + k % NGEO] = 1
        tap[k] = k // NGEO
    for j in range(9 * NSOIL):
        sel[KSOIL + j, j % NSOIL] = 1
        tap[KSOIL + j] = j // NSOIL
    return sel, tap


def table_kernel(sel_ref, tap_ref, soil_ref, geo_ref, weight_ref, table_ref):
    sel = sel_ref[...].astype(bf16)
    embed = jnp.dot(sel[:, :NSOIL], soil_ref[...], preferred_element_type=f32)
    embed = embed + jnp.dot(sel[:, NSOIL:], geo_ref[...], preferred_element_type=f32)
    tap = tap_ref[...]
    total = jnp.zeros((LANES, KROWS), f32)
    for t in range(9):
        mine = jnp.where(tap == t, embed, 0.0).astype(bf16)
        total = total + lax.dot_general(
            weight_ref[t], mine, (((0,), (1,)), ((), ())), preferred_element_type=f32
        )
    high = total.astype(bf16)
    table_ref[0:LANES, :] = high
    table_ref[LANES : 2 * LANES, :] = (total - high.astype(f32)).astype(bf16)


def columns(soil, geo, land, river, elev, rough, rain, evap, head):
    landf = land.astype(f32)
    conveyance = landf * (1.0 + river.astype(f32)) * rough
    return (
        [conveyance, rain, evap, elev, head],
        [(soil + 1).astype(f32), (geo + 1).astype(f32)],
    )


def pack_cols_kernel(
    soil, geo, land, river, elev, rough, rain, evap, head, press, stor, a_ref, b_ref
):
    odd = lax.axis_index("gy") % 2 == 1
    plain, classes = columns(
        soil[...], geo[...], land[...], river[...], elev[...], rough[...], rain[...], evap[...], head[...]
    )
    plain = [press[0], press[1], stor[0], stor[1]] + plain
    width = plain[0].shape[1]
    lane = lax.broadcasted_iota(jnp.int32, (plain[0].shape[0], LANES), 1)

    def side(right):
        halves = []
        for half in range(2):
            acc = jnp.zeros((plain[0].shape[0], LANES), f32)
            items = []
            if half == 0:
                items = [(plain[i], 16, 16 * i) for i in range(8)]
            else:
                items = [(plain[8], 16, 0), (classes[0], 32, 32), (classes[1], 32, 64)]
            for value, wide, at in items:
                part = value[:, width - LANES :] if right else value[:, :LANES]
                start = LANES - wide if right else 0
                moved = part if start == at else pltpu.roll(part, (at - start) % LANES, 1)
                acc = jnp.where((lane >= at) & (lane < at + wide), moved, acc)
            halves.append(acc)
        return halves

    left, right = side(False), side(True)
    for half in range(2):
        cols = slice(half * LANES, (half + 1) * LANES)
        a_ref[:, cols] = jnp.where(odd, left[half], right[half])
        b_ref[:, cols] = jnp.where(odd, right[half], left[half])


def slice_kernel(
    soil, geo, land, river, elev, rough, rain, evap, head, press, stor, z_ref, c_ref, work_ref
):
    plain, classes = columns(
        soil[...], geo[...], land[...], river[...], elev[...], rough[...], rain[...], evap[...], head[...]
    )
    plain = [press[0], press[1], stor[0], stor[1]] + plain
    rows, width = plain[0].shape
    lane = lax.broadcasted_iota(jnp.int32, (rows, LANES), 1)

    def slices(value):
        first, last = value[:, :LANES], value[:, width - LANES :]
        low_r, high_r = pltpu.roll(first, EDGE, 1), pltpu.roll(last, EDGE, 1)
        low_l, high_l = pltpu.roll(first, LANES - EDGE, 1), pltpu.roll(last, LANES - EDGE, 1)
        return [
            jnp.where(lane < EDGE, 0.0, low_r),
            jnp.where(lane < LANES - EDGE, low_l, high_l),
            jnp.where(lane < EDGE, low_r, high_r),
            jnp.where(lane < LANES - EDGE, high_l, 0.0),
        ]

    for i in range(4):
        for d, part in enumerate(slices(plain[i])):
            z_ref[d, i] = part
    for j, value in enumerate(plain[4:] + classes):
        for d, part in enumerate(slices(value)):
            work_ref[d, j] = part
    c_ref[...] = work_ref[lax.axis_index("sec")]


def halo_kernel(z_in, c_in, a_ref, b_ref, z_ref, c_ref, ca_ref, cb_ref):
    odd = lax.axis_index("gy") % 2 == 1
    sec = lax.axis_index("sec")
    rows = c_in.shape[1]
    lane = lax.broadcasted_iota(jnp.int32, (rows, LANES), 1)
    got_a, got_b = a_ref[...], b_ref[...]
    left = jnp.where(odd, got_a, got_b)
    right = jnp.where(odd, got_b, got_a)

    def halos(half, at, wide):
        cols = slice(half * LANES, (half + 1) * LANES)
        lo, hi = left[:, cols], right[:, cols]
        move = (EDGE - wide - at) % LANES
        lo = pltpu.roll(lo, move, 1) if move else lo
        move = (LANES - EDGE - at) % LANES
        hi = pltpu.roll(hi, move, 1) if move else hi
        return (
            jnp.where((lane >= EDGE - wide) & (lane < EDGE), lo, 0.0),
            jnp.where((lane >= LANES - EDGE) & (lane < LANES - EDGE + wide), hi, 0.0),
        )

    inner_l, inner_r = lane >= EDGE, lane < LANES - EDGE
    for i in range(4):
        lo, hi = halos(0, 16 * i, 16)
        z_ref[0, i] = jnp.where(inner_l, z_in[0, i], lo)
        z_ref[1, i] = z_in[1, i]
        z_ref[2, i] = z_in[2, i]
        z_ref[3, i] = jnp.where(inner_r, z_in[3, i], hi)
    spots = [(0, 16 * i, 16) for i in range(4, 8)] + [(1, 0, 16), (1, 32, 32), (1, 64, 32)]
    for j, spot in enumerate(spots):
        lo, hi = halos(*spot)
        value = c_in[j]
        value = jnp.where(inner_l | (sec != 0), value, lo)
        c_ref[j] = jnp.where(inner_r | (sec != 3), value, hi)
    odd_x = lax.axis_index("gx") % 2 == 1
    low = jnp.where(odd_x, rows - HALO, 0)
    low_class = jnp.where(odd_x, rows - CROWS, 0)
    for ref, at, at_class in (
        (ca_ref, low, low_class),
        (cb_ref, (rows - HALO) - low, (rows - CROWS) - low_class),
    ):
        for j in range(5):
            ref[j * HALO : (j + 1) * HALO, :] = c_ref[j, pl.ds(pl.multiple_of(at, 8), HALO), :]
        for j in range(2):
            to = 5 * HALO + j * CROWS
            ref[to : to + CROWS, :] = c_ref[5 + j, pl.ds(pl.multiple_of(at_class, 8), CROWS), :]


def pack_rows_kernel(z_ref, a_ref, b_ref):
    odd = lax.axis_index("gx") % 2 == 1
    rows = z_ref.shape[2]
    low = jnp.where(odd, rows - HALO, 0)
    lane = lax.broadcasted_iota(jnp.int32, (HALO, LANES), 1)
    free = (lane < EDGE - HALO) | (lane >= LANES - EDGE + HALO)
    for ref, at in ((a_ref, low), (b_ref, (rows - HALO) - low)):
        at = pl.multiple_of(at, 8)
        for s in range(4):
            last = z_ref[s, 3, pl.ds(at, HALO), :]
            for i in range(3):
                k = (3 * s + i) * HALO
                moved = pltpu.roll(last, LANES - EDGE * (i + 1), 1)
                ref[k : k + HALO, :] = jnp.where(free, moved, z_ref[s, i, pl.ds(at, HALO), :])


def unpack(ref, s):
    lane = lax.broadcasted_iota(jnp.int32, (HALO, LANES), 1)
    parts = [ref[(3 * s + i) * HALO : (3 * s + i + 1) * HALO, :] for i in range(3)]
    last = jnp.zeros((HALO, LANES), f32)
    for i, part in enumerate(parts):
        start = EDGE - HALO + EDGE * i
        last = jnp.where((lane >= start) & (lane < start + EDGE), pltpu.roll(part, EDGE * (i + 1), 1), last)
    return parts + [last]


MSG_ROWS = 12 * HALO
MSG_ROWS_2D = 5 * HALO + 2 * CROWS


def at_row(r):
    return pl.ds(pl.multiple_of(8 * r + 8, 8), 8)


def shift_classes(ref, kind, value):
    for dx in (-1, 0, 1):
        ref[3 * kind + dx + 1, :, :] = (pltpu.roll(value, (-dx) % LANES, 1) if dx else value) - 1.0


def one_hot(shift_ref, row):
    sub = lax.broadcasted_iota(jnp.int32, (8, LANES), 0)
    low = sub.astype(f32)
    high = low + 8.0
    mid = jnp.where(sub < 4, sub + 8, sub - 4).astype(f32)
    late = low + 4.0
    first4 = sub < 4

    def spread(kind, t):
        dy, dx = t // 3 - 1, t % 3
        return jnp.broadcast_to(shift_ref[3 * kind + dx, pl.ds(row + dy, 1), :], (8, LANES))

    tiles = []
    for t in range(9):
        value = spread(1, t)
        tiles += [value == low, value == high]
    soils = [spread(0, t) for t in range(9)]
    for t in range(0, 9, 2):
        after = soils[t + 1] if t < 8 else jnp.full((8, LANES), -9.0, f32)
        tiles += [soils[t] == low, jnp.where(first4, soils[t], after) == mid]
        if t < 8:
            tiles.append(after == late)
    pairs = [
        jnp.concatenate([jnp.where(a, 1.0, 0.0), jnp.where(b, 1.0, 0.0)], axis=0).astype(bf16)
        for a, b in zip(tiles[0::2], tiles[1::2])
    ]
    return jnp.concatenate(pairs, axis=0)


def conduct_rows(shift_ref, at, count, table, proj):
    hot = jnp.concatenate([one_hot(shift_ref, at + k) for k in range(count)], axis=1)
    both = jnp.dot(table, hot, preferred_element_type=f32)
    hidden = jnp.maximum(both[:LANES] + both[LANES:], 0.0).astype(bf16)
    value = jnp.exp(jnp.dot(proj, hidden, preferred_element_type=f32))
    out = []
    for k in range(count):
        inside = jnp.broadcast_to(shift_ref[1, pl.ds(at + k, 1), :], (8, LANES)) >= 0.0
        out.append(jnp.where(inside, value[:, k * LANES : (k + 1) * LANES], 0.0))
    return out


def by_side(a_ref, b_ref):
    odd = lax.axis_index("gx") % 2 == 1
    a, b = a_ref[...], b_ref[...]
    return jnp.where(odd, b, a), jnp.where(odd, a, b)


def conduct_kernel(c_ref, ca_ref, cb_ref, table_ref, proj_ref, cond_ref, shift_ref):
    full = c_ref.shape[1] + 2 * HALO
    above, below = by_side(ca_ref, cb_ref)
    for kind in range(2):
        at = 5 * HALO + kind * CROWS
        value = jnp.concatenate([above[at : at + CROWS], c_ref[5 + kind], below[at : at + CROWS]], axis=0)
        shift_classes(shift_ref, kind, value)
    table, proj = table_ref[...], proj_ref[...]

    for row in range(0, full, full // 2):
        for k, value in enumerate(conduct_rows(shift_ref, row + CROWS - HALO, full // 2, table, proj)):
            cond_ref[at_row(row + k), :] = value
    cond_ref[0:8, :] = jnp.zeros((8, LANES), f32)
    cond_ref[8 * (full + 1) :, :] = jnp.zeros((8, LANES), f32)


def face_coefficients(cond_ref, r, store):
    sub = lax.broadcasted_iota(jnp.int32, (8, LANES), 0)
    mid = cond_ref[at_row(r), :]
    north = 0.5 * lateral * (mid + cond_ref[at_row(r - 1), :])
    south = 0.5 * lateral * (mid + cond_ref[at_row(r + 1), :])
    east = 0.5 * lateral * (mid + pltpu.roll(mid, LANES - 1, 1))
    west = pltpu.roll(east, 1, 1)
    up = 0.5 * vertical * (mid + jnp.where(sub > 0, pltpu.roll(mid, 1, 0), 0.0))
    down = 0.5 * vertical * (mid + jnp.where(sub < 7, pltpu.roll(mid, 7, 0), 0.0))
    diagonal = store + up + down + north + south + east + west
    live = store > 0.0
    inverse = jnp.where(live, 1.0, 0.0) / jnp.where(live, diagonal, 1.0)
    return (
        jnp.where(sub > 0, up * inverse, 0.0),
        jnp.where(sub < 7, down * inverse, 0.0),
        north * inverse,
        south * inverse,
        east * inverse,
        west * inverse,
        store * inverse,
        jnp.where(sub == 0, inverse, 0.0),
    )


def by_layer(parts):
    return jnp.swapaxes(jnp.stack(parts), 0, 1).reshape(64, LANES)


def own_kernel(z_ref, cond_ref, press_ref, coef_ref):
    rows = z_ref.shape[2]
    for r in range(0, rows, 8):
        press_ref[8 * r : 8 * r + 64, :] = by_layer([z_ref[l // 2, l % 2, r : r + 8, :] for l in range(8)])
        store = by_layer([z_ref[l // 2, 2 + l % 2, r : r + 8, :] for l in range(8)])
        for i in range(8):
            values = face_coefficients(cond_ref, r + i + HALO, store[8 * i : 8 * i + 8])
            for k, value in enumerate(values):
                coef_ref[k, 8 * (r + i) : 8 * (r + i) + 8, :] = value


def main_kernel(
    c_ref, ca_ref, cb_ref, a_ref, b_ref, cond_ref, own_press_ref, own_coef_ref, out_ref,
    press_ref, press2_ref, coef_ref, rhs_ref, flat_ref, src_ref,
):
    rows = c_ref.shape[1]
    full = rows + 2 * HALO
    above, below = by_side(ca_ref, cb_ref)

    def edge_row(r):
        at = 8 * (r if r < HALO else r - rows)
        return slice(at, at + 8)

    for j in range(5):
        at = j * HALO
        flat_ref[j, 0:HALO, :] = above[at : at + HALO]
        flat_ref[j, HALO : HALO + rows, :] = c_ref[j]
        flat_ref[j, HALO + rows : full, :] = below[at : at + HALO]

    press_ref[8 * (HALO + 1) : 8 * (HALO + rows + 1), :] = own_press_ref[...]
    for side, low in zip(by_side(a_ref, b_ref), (0, HALO + rows)):
        fields = [unpack(side, s) for s in range(4)]
        for r in range(0, HALO, 8):
            at = 8 * (low + r + 1)
            press_ref[at : at + 64, :] = by_layer([fields[l // 2][l % 2][r : r + 8] for l in range(8)])
            store = by_layer([fields[l // 2][2 + l % 2][r : r + 8] for l in range(8)])
            for i in range(8):
                row = low + r + i
                if 0 < row < full - 1:
                    values = face_coefficients(cond_ref, row, store[8 * i : 8 * i + 8])
                    for k, value in enumerate(values):
                        coef_ref[k, edge_row(row), :] = value

    def coef(k, r):
        if HALO <= r < HALO + rows:
            return own_coef_ref[k, 8 * (r - HALO) : 8 * (r - HALO) + 8, :]
        return coef_ref[k, edge_row(r), :]

    rough, rain, evap, elev = flat_ref[0], flat_ref[1], flat_ref[2], flat_ref[3]
    head = flat_ref[4]
    land = jnp.where(rough > 0.0, 1.0, 0.0)

    def around(value):
        return (
            pltpu.roll(value, full - 1, 0),
            pltpu.roll(value, 1, 0),
            pltpu.roll(value, LANES - 1, 1),
            pltpu.roll(value, 1, 1),
        )

    faces = [0.5 * (rough + near) for near in around(rough)]
    top_cond = cond_ref[pl.ds(8, full, stride=8), :]
    rate = land * (infil_rate * top_cond / (1.0 + top_cond))
    loss = land * evap
    for cycle in range(CYCLES):
        top = press_ref[pl.ds(8, full, stride=8), :]
        level = head + elev
        flux = jnp.zeros_like(level)
        for face, near in zip(faces, around(level)):
            flux = flux + face * (near - level)
        infil = rate * (head - top)
        src_ref[...] = infil - loss * jax.nn.sigmoid(top)
        head = head + land * (rain - infil + flux)
        done = cycle * SWEEPS

        for sweep in range(SWEEPS):
            old, new = (press_ref, press2_ref) if sweep % 2 == 0 else (press2_ref, press_ref)

            for r in range(done + sweep + 1, full - done - sweep - 1):
                here = slice(8 * r, 8 * r + 8)
                mid = old[at_row(r), :]
                if sweep == 0:
                    source = jnp.broadcast_to(src_ref[r : r + 1, :], (8, LANES))
                    rhs = coef(6, r) * mid + coef(7, r) * source
                    rhs_ref[here, :] = rhs
                else:
                    rhs = rhs_ref[here, :]
                column = coef(0, r) * pltpu.roll(mid, 1, 0) + coef(1, r) * pltpu.roll(mid, 7, 0)
                across = coef(2, r) * old[at_row(r - 1), :] + coef(3, r) * old[at_row(r + 1), :]
                along = coef(4, r) * pltpu.roll(mid, LANES - 1, 1) + coef(5, r) * pltpu.roll(mid, 1, 1)
                new[at_row(r), :] = (rhs + column) + (across + along)

    lane = lax.broadcasted_iota(jnp.int32, (8, LANES), 1)
    for r in range(HALO, HALO + rows, 8):
        layers = jnp.swapaxes(press_ref[8 * (r + 1) : 8 * (r + 9), :].reshape(8, 8, LANES), 0, 1)
        for s in range(4):
            out_ref[s, r - HALO : r - HALO + 8, :] = jnp.where(
                lane < CHUNK,
                pltpu.roll(layers[2 * s], LANES - EDGE, 1),
                pltpu.roll(layers[2 * s + 1], EDGE, 1),
            )
    for r in range(HALO, HALO + rows // 2, 8):
        both = jnp.where(
            lane < CHUNK,
            pltpu.roll(head[r : r + 8], LANES - EDGE, 1),
            pltpu.roll(head[r + rows // 2 : r + rows // 2 + 8], EDGE, 1),
        )
        for s in range(4):
            out_ref[s, rows + r - HALO : rows + r - HALO + 8, :] = both


def finish_kernel(z_ref, press_ref, head_ref):
    rows = head_ref.shape[0]
    half = rows // 2
    lane = lax.broadcasted_iota(jnp.int32, (rows, LANES), 1)
    low = lane[:half] < CHUNK
    for d in range(0, 4, 2):
        cols = slice(d * CHUNK, d * CHUNK + LANES)
        a, b = z_ref[d, :rows, :], z_ref[d + 1, :rows, :]
        press_ref[0, :, cols] = jnp.where(lane < CHUNK, a, pltpu.roll(b, CHUNK, 1))
        press_ref[1, :, cols] = jnp.where(lane < CHUNK, pltpu.roll(a, CHUNK, 1), b)
        a, b = z_ref[d, rows:, :], z_ref[d + 1, rows:, :]
        head_ref[:half, cols] = jnp.where(low, a, pltpu.roll(b, CHUNK, 1))
        head_ref[half:, cols] = jnp.where(low, pltpu.roll(a, CHUNK, 1), b)


def main_call(rows, args):
    full = rows + 2 * HALO
    grid = (8 * full, LANES)
    framed = (8 * (full + 2), LANES)
    return call(
        main_kernel, (jax.ShapeDtypeStruct((4, rows + rows // 2, LANES), f32),), args,
        scratch=[
            pltpu.VMEM(framed, f32),
            pltpu.VMEM(framed, f32),
            pltpu.VMEM((8, 8 * 2 * HALO, LANES), f32),
            pltpu.VMEM(grid, f32),
            pltpu.VMEM((5, full, LANES), f32),
            pltpu.VMEM((full, LANES), f32),
        ],
    )[0]


def shards(
    soil_class, geology_class, land_mask, river_mask, elevation, roughness, rainfall, potential_evap,
    surface_head, pressure, storage, soil_embed, geology_embed, conv_weight, out_weight,
):
    rows, width = soil_class.shape
    n_gx, n_gy = lax.axis_size("gx"), lax.axis_size("gy")
    sds = jax.ShapeDtypeStruct
    raw = (
        soil_class, geology_class, land_mask, river_mask, elevation, roughness, rainfall,
        potential_evap, surface_head, pressure, storage,
    )
    given = tuple(range(len(raw)))

    edge = sds((rows, 2 * LANES), f32)
    chunks, plane = sds((4, 4, rows, LANES), f32), sds((7, rows, LANES), f32)
    ya, yb = call(pack_cols_kernel, (edge, edge), raw, hbm=given)
    ya, yb, head = lax.optimization_barrier((ya, yb, surface_head))
    ya = lax.ppermute(ya, "gy", swap_pairs(n_gy, 0))
    yb = lax.ppermute(yb, "gy", swap_pairs(n_gy, 1))

    z, cols = call(
        slice_kernel, (chunks, plane), (*raw[:8], head, *raw[9:]),
        scratch=[pltpu.VMEM((4, 7, rows, LANES), f32)], hbm=given,
    )
    ya, yb, z, cols = lax.optimization_barrier((ya, yb, z, cols))
    edge_2d = sds((MSG_ROWS_2D, LANES), f32)
    z, cols, ca, cb = call(halo_kernel, (chunks, plane, edge_2d, edge_2d), (z, cols, ya, yb))
    z = lax.all_to_all(z, "sec", 0, 0)

    cb = lax.ppermute(cb, "gx", swap_pairs(n_gx, 0))
    ca = lax.ppermute(ca, "gx", swap_pairs(n_gx, 1))

    msg = sds((MSG_ROWS, LANES), f32)
    xa, xb = call(pack_rows_kernel, (msg, msg), (z,))
    xa, xb, cols, soil_embed = lax.optimization_barrier((xa, xb, cols, soil_embed))
    xa = lax.ppermute(xa, "gx", swap_pairs(n_gx, 1))
    xb = lax.ppermute(xb, "gx", swap_pairs(n_gx, 0))

    sel, tap = table_layout()
    (table,) = call(
        table_kernel, (sds((2 * LANES, KROWS), bf16),),
        (
            jnp.asarray(sel), jnp.asarray(tap), soil_embed, geology_embed,
            conv_weight.reshape(9, LANES, LANES),
        ),
        hbm=range(5),
    )
    (cond,) = call(
        conduct_kernel, (sds((8 * (rows + 2 * HALO + 2), LANES), f32),), (cols, ca, cb, table, out_weight.T),
        scratch=[pltpu.VMEM((6, rows + 2 * CROWS, LANES), f32)], hbm=(4,),
    )
    own_press, own_coef = call(own_kernel, (sds((8 * rows, LANES), f32), sds((8, 8 * rows, LANES), f32)), (z, cond))
    xa, xb, own_press, own_coef = lax.optimization_barrier((xa, xb, own_press, own_coef))
    out = main_call(rows, (cols, ca, cb, xa, xb, cond, own_press, own_coef))
    out = lax.all_to_all(out, "sec", 0, 0)
    return call(finish_kernel, (sds(pressure.shape, f32), sds((rows, width), f32)), (out,), final=True)


def solution(mesh):
    flat = P("gx", "gy")
    deep = P("sec", "gx", "gy")
    in_specs = (flat,) * 9 + (deep, deep) + (P(),) * 4
    return jax.shard_map(shards, mesh=mesh, in_specs=in_specs, out_specs=(deep, flat), check_vma=False)
```

```python
import jax
import jax.numpy as jnp
import numpy as np
from jax import lax
from jax.experimental import pallas as pl
from jax.experimental.pallas import tpu as pltpu
from jax.sharding import PartitionSpec as P


SWEEPS = 4
CYCLES = 4
HALO = SWEEPS * CYCLES
LANES = 128
CHUNK = 64
EDGE = (LANES - CHUNK) // 2
CROWS = 24
NSOIL = 12
NGEO = 16
KSOIL = 9 * NGEO
KROWS = 256

infil_rate = 0.3
lateral = 1.0
vertical = 0.5

VMEM = pl.BlockSpec(memory_space=pltpu.VMEM)
f32 = jnp.float32
bf16 = jnp.bfloat16


def call(kernel, outs, args, scratch=(), hbm=(), final=False):
    made = outs if final else tuple(pltpu.VMEM(o.shape, o.dtype) for o in outs)
    args = [x if i in hbm else pltpu.with_memory_space_constraint(x, pltpu.VMEM) for i, x in enumerate(args)]
    return pl.pallas_call(
        kernel, out_shape=made, in_specs=[VMEM] * len(args), out_specs=tuple(VMEM for _ in outs), scratch_shapes=scratch
    )(*args)


def swap_pairs(count, first):
    out = []
    for i in range(first, count - 1, 2):
        out += [(i, i + 1), (i + 1, i)]
    return out


def table_layout():
    sel = np.zeros((KROWS, NSOIL + NGEO), np.float32)
    tap = np.full((KROWS, LANES), -1, np.int32)
    for k in range(KSOIL):
        sel[k, NSOIL + k % NGEO] = 1
        tap[k] = k // NGEO
    for j in range(9 * NSOIL):
        sel[KSOIL + j, j % NSOIL] = 1
        tap[KSOIL + j] = j // NSOIL
    return sel, tap


def table_kernel(sel_ref, tap_ref, soil_ref, geo_ref, weight_ref, table_ref):
    sel = sel_ref[...].astype(bf16)
    embed = jnp.dot(sel[:, :NSOIL], soil_ref[...], preferred_element_type=f32)
    embed = embed + jnp.dot(sel[:, NSOIL:], geo_ref[...], preferred_element_type=f32)
    tap = tap_ref[...]
    total = jnp.zeros((LANES, KROWS), f32)
    for t in range(9):
        mine = jnp.where(tap == t, embed, 0.0).astype(bf16)
        total = total + lax.dot_general(
            weight_ref[t], mine, (((0,), (1,)), ((), ())), preferred_element_type=f32
        )
    high = total.astype(bf16)
    table_ref[0:LANES, :] = high
    table_ref[LANES : 2 * LANES, :] = (total - high.astype(f32)).astype(bf16)


def columns(soil, geo, land, river, elev, rough, rain, evap, head):
    landf = land.astype(f32)
    conveyance = landf * (1.0 + river.astype(f32)) * rough
    return (
        [conveyance, rain, evap, elev, head],
        [(soil + 1).astype(f32), (geo + 1).astype(f32)],
    )


def pack_cols_kernel(
    soil, geo, land, river, elev, rough, rain, evap, head, press, stor, a_ref, b_ref
):
    odd = lax.axis_index("gy") % 2 == 1
    plain, classes = columns(
        soil[...], geo[...], land[...], river[...], elev[...], rough[...], rain[...], evap[...], head[...]
    )
    plain = [press[0], press[1], stor[0], stor[1]] + plain
    width = plain[0].shape[1]
    lane = lax.broadcasted_iota(jnp.int32, (plain[0].shape[0], LANES), 1)

    def side(right):
        halves = []
        for half in range(2):
            acc = jnp.zeros((plain[0].shape[0], LANES), f32)
            items = []
            if half == 0:
                items = [(plain[i], 16, 16 * i) for i in range(8)]
            else:
                items = [(plain[8], 16, 0), (classes[0], 32, 32), (classes[1], 32, 64)]
            for value, wide, at in items:
                part = value[:, width - LANES :] if right else value[:, :LANES]
                start = LANES - wide if right else 0
                moved = part if start == at else pltpu.roll(part, (at - start) % LANES, 1)
                acc = jnp.where((lane >= at) & (lane < at + wide), moved, acc)
            halves.append(acc)
        return halves

    left, right = side(False), side(True)
    for half in range(2):
        cols = slice(half * LANES, (half + 1) * LANES)
        a_ref[:, cols] = jnp.where(odd, left[half], right[half])
        b_ref[:, cols] = jnp.where(odd, right[half], left[half])


def slice_kernel(
    soil, geo, land, river, elev, rough, rain, evap, head, press, stor, z_ref, c_ref, work_ref
):
    plain, classes = columns(
        soil[...], geo[...], land[...], river[...], elev[...], rough[...], rain[...], evap[...], head[...]
    )
    plain = [press[0], press[1], stor[0], stor[1]] + plain
    rows, width = plain[0].shape
    lane = lax.broadcasted_iota(jnp.int32, (rows, LANES), 1)

    def slices(value):
        first, last = value[:, :LANES], value[:, width - LANES :]
        low_r, high_r = pltpu.roll(first, EDGE, 1), pltpu.roll(last, EDGE, 1)
        low_l, high_l = pltpu.roll(first, LANES - EDGE, 1), pltpu.roll(last, LANES - EDGE, 1)
        return [
            jnp.where(lane < EDGE, 0.0, low_r),
            jnp.where(lane < LANES - EDGE, low_l, high_l),
            jnp.where(lane < EDGE, low_r, high_r),
            jnp.where(lane < LANES - EDGE, high_l, 0.0),
        ]

    for i in range(4):
        for d, part in enumerate(slices(plain[i])):
            z_ref[d, i] = part
    for j, value in enumerate(plain[4:] + classes):
        for d, part in enumerate(slices(value)):
            work_ref[d, j] = part
    c_ref[...] = work_ref[lax.axis_index("sec")]


def halo_kernel(z_in, c_in, a_ref, b_ref, z_ref, c_ref, ca_ref, cb_ref):
    odd = lax.axis_index("gy") % 2 == 1
    sec = lax.axis_index("sec")
    rows = c_in.shape[1]
    lane = lax.broadcasted_iota(jnp.int32, (rows, LANES), 1)
    got_a, got_b = a_ref[...], b_ref[...]
    left = jnp.where(odd, got_a, got_b)
    right = jnp.where(odd, got_b, got_a)

    def halos(half, at, wide):
        cols = slice(half * LANES, (half + 1) * LANES)
        lo, hi = left[:, cols], right[:, cols]
        move = (EDGE - wide - at) % LANES
        lo = pltpu.roll(lo, move, 1) if move else lo
        move = (LANES - EDGE - at) % LANES
        hi = pltpu.roll(hi, move, 1) if move else hi
        return (
            jnp.where((lane >= EDGE - wide) & (lane < EDGE), lo, 0.0),
            jnp.where((lane >= LANES - EDGE) & (lane < LANES - EDGE + wide), hi, 0.0),
        )

    inner_l, inner_r = lane >= EDGE, lane < LANES - EDGE
    fields = []
    for i in range(4):
        lo, hi = halos(0, 16 * i, 16)
        fields.append(
            (jnp.where(inner_l, z_in[0, i], lo), z_in[1, i], z_in[2, i], jnp.where(inner_r, z_in[3, i], hi))
        )
    free = (lane < EDGE - HALO) | (lane >= LANES - EDGE + HALO)
    for d in range(4):
        for i in range(3):
            moved = pltpu.roll(fields[3][d], LANES - EDGE * (i + 1), 1)
            z_ref[d, i] = jnp.where(free, moved, fields[i][d])
    spots = [(0, 16 * i, 16) for i in range(4, 8)] + [(1, 0, 16), (1, 32, 32), (1, 64, 32)]
    for j, spot in enumerate(spots):
        lo, hi = halos(*spot)
        value = c_in[j]
        value = jnp.where(inner_l | (sec != 0), value, lo)
        c_ref[j] = jnp.where(inner_r | (sec != 3), value, hi)
    odd_x = lax.axis_index("gx") % 2 == 1
    low = jnp.where(odd_x, rows - HALO, 0)
    low_class = jnp.where(odd_x, rows - CROWS, 0)
    for ref, at, at_class in (
        (ca_ref, low, low_class),
        (cb_ref, (rows - HALO) - low, (rows - CROWS) - low_class),
    ):
        for j in range(5):
            ref[j * HALO : (j + 1) * HALO, :] = c_ref[j, pl.ds(pl.multiple_of(at, 8), HALO), :]
        for j in range(2):
            to = 5 * HALO + j * CROWS
            ref[to : to + CROWS, :] = c_ref[5 + j, pl.ds(pl.multiple_of(at_class, 8), CROWS), :]


def pack_rows_kernel(z_ref, a_ref, b_ref):
    odd = lax.axis_index("gx") % 2 == 1
    rows = z_ref.shape[2]
    low = jnp.where(odd, rows - HALO, 0)
    for ref, at in ((a_ref, low), (b_ref, (rows - HALO) - low)):
        at = pl.multiple_of(at, 8)
        for s in range(4):
            for i in range(3):
                k = (3 * s + i) * HALO
                ref[k : k + HALO, :] = z_ref[s, i, pl.ds(at, HALO), :]


def unpack(parts):
    lane = lax.broadcasted_iota(jnp.int32, parts[0].shape, 1)
    last = jnp.zeros_like(parts[0])
    for i, part in enumerate(parts):
        start = EDGE - HALO + EDGE * i
        last = jnp.where((lane >= start) & (lane < start + EDGE), pltpu.roll(part, EDGE * (i + 1), 1), last)
    return parts + [last]


MSG_ROWS = 12 * HALO
MSG_ROWS_2D = 5 * HALO + 2 * CROWS


def at_row(r):
    return pl.ds(pl.multiple_of(8 * r + 8, 8), 8)


def shift_classes(ref, kind, value):
    for dx in (-1, 0, 1):
        ref[3 * kind + dx + 1, :, :] = (pltpu.roll(value, (-dx) % LANES, 1) if dx else value) - 1.0


def one_hot(shift_ref, row):
    sub = lax.broadcasted_iota(jnp.int32, (8, LANES), 0)
    low = sub.astype(f32)
    high = low + 8.0
    mid = jnp.where(sub < 4, sub + 8, sub - 4).astype(f32)
    late = low + 4.0
    first4 = sub < 4

    def spread(kind, t):
        dy, dx = t // 3 - 1, t % 3
        return jnp.broadcast_to(shift_ref[3 * kind + dx, pl.ds(row + dy, 1), :], (8, LANES))

    tiles = []
    for t in range(9):
        value = spread(1, t)
        tiles += [value == low, value == high]
    soils = [spread(0, t) for t in range(9)]
    for t in range(0, 9, 2):
        after = soils[t + 1] if t < 8 else jnp.full((8, LANES), -9.0, f32)
        tiles += [soils[t] == low, jnp.where(first4, soils[t], after) == mid]
        if t < 8:
            tiles.append(after == late)
    pairs = [
        jnp.concatenate([jnp.where(a, 1.0, 0.0), jnp.where(b, 1.0, 0.0)], axis=0).astype(bf16)
        for a, b in zip(tiles[0::2], tiles[1::2])
    ]
    return jnp.concatenate(pairs, axis=0)


def conduct_rows(shift_ref, at, count, table, proj):
    hot = jnp.concatenate([one_hot(shift_ref, at + k) for k in range(count)], axis=1)
    both = jnp.dot(table, hot, preferred_element_type=f32)
    hidden = jnp.maximum(both[:LANES] + both[LANES:], 0.0).astype(bf16)
    value = jnp.exp(jnp.dot(proj, hidden, preferred_element_type=f32))
    out = []
    for k in range(count):
        inside = jnp.broadcast_to(shift_ref[1, pl.ds(at + k, 1), :], (8, LANES)) >= 0.0
        out.append(jnp.where(inside, value[:, k * LANES : (k + 1) * LANES], 0.0))
    return out


def by_side(a_ref, b_ref):
    odd = lax.axis_index("gx") % 2 == 1
    a, b = a_ref[...], b_ref[...]
    return jnp.where(odd, b, a), jnp.where(odd, a, b)


def conduct_kernel(c_ref, ca_ref, cb_ref, table_ref, proj_ref, cond_ref, shift_ref):
    full = c_ref.shape[1] + 2 * HALO
    above, below = by_side(ca_ref, cb_ref)
    for kind in range(2):
        at = 5 * HALO + kind * CROWS
        value = jnp.concatenate([above[at : at + CROWS], c_ref[5 + kind], below[at : at + CROWS]], axis=0)
        shift_classes(shift_ref, kind, value)
    table, proj = table_ref[...], proj_ref[...]

    for row in range(0, full, full // 2):
        for k, value in enumerate(conduct_rows(shift_ref, row + CROWS - HALO, full // 2, table, proj)):
            cond_ref[at_row(row + k), :] = value
    cond_ref[0:8, :] = jnp.zeros((8, LANES), f32)
    cond_ref[8 * (full + 1) :, :] = jnp.zeros((8, LANES), f32)


def face_coefficients(cond_ref, r, store):
    sub = lax.broadcasted_iota(jnp.int32, (8, LANES), 0)
    mid = cond_ref[at_row(r), :]
    north = 0.5 * lateral * (mid + cond_ref[at_row(r - 1), :])
    south = 0.5 * lateral * (mid + cond_ref[at_row(r + 1), :])
    east = 0.5 * lateral * (mid + pltpu.roll(mid, LANES - 1, 1))
    west = pltpu.roll(east, 1, 1)
    up = 0.5 * vertical * (mid + jnp.where(sub > 0, pltpu.roll(mid, 1, 0), 0.0))
    down = 0.5 * vertical * (mid + jnp.where(sub < 7, pltpu.roll(mid, 7, 0), 0.0))
    diagonal = store + up + down + north + south + east + west
    live = store > 0.0
    inverse = jnp.where(live, 1.0, 0.0) / jnp.where(live, diagonal, 1.0)
    return (
        jnp.where(sub > 0, up * inverse, 0.0),
        jnp.where(sub < 7, down * inverse, 0.0),
        north * inverse,
        south * inverse,
        east * inverse,
        west * inverse,
        store * inverse,
        jnp.where(sub == 0, inverse, 0.0),
    )


def by_layer(parts):
    return jnp.swapaxes(jnp.stack(parts), 0, 1).reshape(64, LANES)


def own_kernel(z_ref, cond_ref, press_ref, coef_ref):
    rows = z_ref.shape[2]
    for r in range(0, rows, 8):
        fields = [unpack([z_ref[s, i, r : r + 8, :] for i in range(3)]) for s in range(4)]
        press_ref[8 * r : 8 * r + 64, :] = by_layer([fields[l // 2][l % 2] for l in range(8)])
        store = by_layer([fields[l // 2][2 + l % 2] for l in range(8)])
        for i in range(8):
            values = face_coefficients(cond_ref, r + i + HALO, store[8 * i : 8 * i + 8])
            for k, value in enumerate(values):
                coef_ref[k, 8 * (r + i) : 8 * (r + i) + 8, :] = value


def main_kernel(
    c_ref, ca_ref, cb_ref, a_ref, b_ref, cond_ref, own_press_ref, own_coef_ref, out_ref,
    press_ref, press2_ref, coef_ref, rhs_ref, flat_ref, src_ref,
):
    rows = c_ref.shape[1]
    full = rows + 2 * HALO
    above, below = by_side(ca_ref, cb_ref)

    def edge_row(r):
        at = 8 * (r if r < HALO else r - rows)
        return slice(at, at + 8)

    for j in range(5):
        at = j * HALO
        flat_ref[j, 0:HALO, :] = above[at : at + HALO]
        flat_ref[j, HALO : HALO + rows, :] = c_ref[j]
        flat_ref[j, HALO + rows : full, :] = below[at : at + HALO]

    press_ref[8 * (HALO + 1) : 8 * (HALO + rows + 1), :] = own_press_ref[...]
    for side, low in zip(by_side(a_ref, b_ref), (0, HALO + rows)):
        fields = [unpack([side[(3 * s + i) * HALO : (3 * s + i + 1) * HALO] for i in range(3)]) for s in range(4)]
        for r in range(0, HALO, 8):
            at = 8 * (low + r + 1)
            press_ref[at : at + 64, :] = by_layer([fields[l // 2][l % 2][r : r + 8] for l in range(8)])
            store = by_layer([fields[l // 2][2 + l % 2][r : r + 8] for l in range(8)])
            for i in range(8):
                row = low + r + i
                if 0 < row < full - 1:
                    values = face_coefficients(cond_ref, row, store[8 * i : 8 * i + 8])
                    for k, value in enumerate(values):
                        coef_ref[k, edge_row(row), :] = value

    def coef(k, r):
        if HALO <= r < HALO + rows:
            return own_coef_ref[k, 8 * (r - HALO) : 8 * (r - HALO) + 8, :]
        return coef_ref[k, edge_row(r), :]

    rough, rain, evap, elev = flat_ref[0], flat_ref[1], flat_ref[2], flat_ref[3]
    head = flat_ref[4]
    land = jnp.where(rough > 0.0, 1.0, 0.0)

    def around(value):
        return (
            pltpu.roll(value, full - 1, 0),
            pltpu.roll(value, 1, 0),
            pltpu.roll(value, LANES - 1, 1),
            pltpu.roll(value, 1, 1),
        )

    faces = [0.5 * (rough + near) for near in around(rough)]
    top_cond = cond_ref[pl.ds(8, full, stride=8), :]
    rate = land * (infil_rate * top_cond / (1.0 + top_cond))
    loss = land * evap
    for cycle in range(CYCLES):
        top = press_ref[pl.ds(8, full, stride=8), :]
        level = head + elev
        flux = jnp.zeros_like(level)
        for face, near in zip(faces, around(level)):
            flux = flux + face * (near - level)
        infil = rate * (head - top)
        src_ref[...] = infil - loss * jax.nn.sigmoid(top)
        head = head + land * (rain - infil + flux)
        done = cycle * SWEEPS

        for sweep in range(SWEEPS):
            old, new = (press_ref, press2_ref) if sweep % 2 == 0 else (press2_ref, press_ref)

            for r in range(done + sweep + 1, full - done - sweep - 1):
                here = slice(8 * r, 8 * r + 8)
                mid = old[at_row(r), :]
                if sweep == 0:
                    source = jnp.broadcast_to(src_ref[r : r + 1, :], (8, LANES))
                    rhs = coef(6, r) * mid + coef(7, r) * source
                    rhs_ref[here, :] = rhs
                else:
                    rhs = rhs_ref[here, :]
                column = coef(0, r) * pltpu.roll(mid, 1, 0) + coef(1, r) * pltpu.roll(mid, 7, 0)
                across = coef(2, r) * old[at_row(r - 1), :] + coef(3, r) * old[at_row(r + 1), :]
                along = coef(4, r) * pltpu.roll(mid, LANES - 1, 1) + coef(5, r) * pltpu.roll(mid, 1, 1)
                new[at_row(r), :] = (rhs + column) + (across + along)

    lane = lax.broadcasted_iota(jnp.int32, (8, LANES), 1)
    for r in range(HALO, HALO + rows, 8):
        layers = jnp.swapaxes(press_ref[8 * (r + 1) : 8 * (r + 9), :].reshape(8, 8, LANES), 0, 1)
        for s in range(4):
            out_ref[s, r - HALO : r - HALO + 8, :] = jnp.where(
                lane < CHUNK,
                pltpu.roll(layers[2 * s], LANES - EDGE, 1),
                pltpu.roll(layers[2 * s + 1], EDGE, 1),
            )
    for r in range(HALO, HALO + rows // 2, 8):
        both = jnp.where(
            lane < CHUNK,
            pltpu.roll(head[r : r + 8], LANES - EDGE, 1),
            pltpu.roll(head[r + rows // 2 : r + rows // 2 + 8], EDGE, 1),
        )
        for s in range(4):
            out_ref[s, rows + r - HALO : rows + r - HALO + 8, :] = both


def finish_kernel(z_ref, press_ref, head_ref):
    rows = head_ref.shape[0]
    half = rows // 2
    lane = lax.broadcasted_iota(jnp.int32, (rows, LANES), 1)
    low = lane[:half] < CHUNK
    for d in range(0, 4, 2):
        cols = slice(d * CHUNK, d * CHUNK + LANES)
        a, b = z_ref[d, :rows, :], z_ref[d + 1, :rows, :]
        press_ref[0, :, cols] = jnp.where(lane < CHUNK, a, pltpu.roll(b, CHUNK, 1))
        press_ref[1, :, cols] = jnp.where(lane < CHUNK, pltpu.roll(a, CHUNK, 1), b)
        a, b = z_ref[d, rows:, :], z_ref[d + 1, rows:, :]
        head_ref[:half, cols] = jnp.where(low, a, pltpu.roll(b, CHUNK, 1))
        head_ref[half:, cols] = jnp.where(low, pltpu.roll(a, CHUNK, 1), b)


def main_call(rows, args):
    full = rows + 2 * HALO
    grid = (8 * full, LANES)
    framed = (8 * (full + 2), LANES)
    return call(
        main_kernel, (jax.ShapeDtypeStruct((4, rows + rows // 2, LANES), f32),), args,
        scratch=[
            pltpu.VMEM(framed, f32),
            pltpu.VMEM(framed, f32),
            pltpu.VMEM((8, 8 * 2 * HALO, LANES), f32),
            pltpu.VMEM(grid, f32),
            pltpu.VMEM((5, full, LANES), f32),
            pltpu.VMEM((full, LANES), f32),
        ],
    )[0]


def shards(
    soil_class, geology_class, land_mask, river_mask, elevation, roughness, rainfall, potential_evap,
    surface_head, pressure, storage, soil_embed, geology_embed, conv_weight, out_weight,
):
    rows, width = soil_class.shape
    n_gx, n_gy = lax.axis_size("gx"), lax.axis_size("gy")
    sds = jax.ShapeDtypeStruct
    raw = (
        soil_class, geology_class, land_mask, river_mask, elevation, roughness, rainfall,
        potential_evap, surface_head, pressure, storage,
    )
    given = tuple(range(len(raw)))

    edge = sds((rows, 2 * LANES), f32)
    chunks, plane = sds((4, 4, rows, LANES), f32), sds((7, rows, LANES), f32)
    ya, yb = call(pack_cols_kernel, (edge, edge), raw, hbm=given)
    ya, yb, head = lax.optimization_barrier((ya, yb, surface_head))
    ya = lax.ppermute(ya, "gy", swap_pairs(n_gy, 0))
    yb = lax.ppermute(yb, "gy", swap_pairs(n_gy, 1))

    z, cols = call(
        slice_kernel, (chunks, plane), (*raw[:8], head, *raw[9:]),
        scratch=[pltpu.VMEM((4, 7, rows, LANES), f32)], hbm=given,
    )
    ya, yb, z, cols = lax.optimization_barrier((ya, yb, z, cols))
    edge_2d = sds((MSG_ROWS_2D, LANES), f32)
    z, cols, ca, cb = call(halo_kernel, (sds((4, 3, rows, LANES), f32), plane, edge_2d, edge_2d), (z, cols, ya, yb))
    z = lax.all_to_all(z, "sec", 0, 0)

    cb = lax.ppermute(cb, "gx", swap_pairs(n_gx, 0))
    ca = lax.ppermute(ca, "gx", swap_pairs(n_gx, 1))

    msg = sds((MSG_ROWS, LANES), f32)
    xa, xb = call(pack_rows_kernel, (msg, msg), (z,))
    xa, xb, cols, soil_embed = lax.optimization_barrier((xa, xb, cols, soil_embed))
    xa = lax.ppermute(xa, "gx", swap_pairs(n_gx, 1))
    xb = lax.ppermute(xb, "gx", swap_pairs(n_gx, 0))

    sel, tap = table_layout()
    (table,) = call(
        table_kernel, (sds((2 * LANES, KROWS), bf16),),
        (
            jnp.asarray(sel), jnp.asarray(tap), soil_embed, geology_embed,
            conv_weight.reshape(9, LANES, LANES),
        ),
        hbm=range(5),
    )
    (cond,) = call(
        conduct_kernel, (sds((8 * (rows + 2 * HALO + 2), LANES), f32),), (cols, ca, cb, table, out_weight.T),
        scratch=[pltpu.VMEM((6, rows + 2 * CROWS, LANES), f32)], hbm=(4,),
    )
    own_press, own_coef = call(own_kernel, (sds((8 * rows, LANES), f32), sds((8, 8 * rows, LANES), f32)), (z, cond))
    xa, xb, own_press, own_coef = lax.optimization_barrier((xa, xb, own_press, own_coef))
    out = main_call(rows, (cols, ca, cb, xa, xb, cond, own_press, own_coef))
    out = lax.all_to_all(out, "sec", 0, 0)
    return call(finish_kernel, (sds(pressure.shape, f32), sds((rows, width), f32)), (out,), final=True)


def solution(mesh):
    flat = P("gx", "gy")
    deep = P("sec", "gx", "gy")
    in_specs = (flat,) * 9 + (deep, deep) + (P(),) * 4
    return jax.shard_map(shards, mesh=mesh, in_specs=in_specs, out_specs=(deep, flat), check_vma=False)
```
